128 devices in a mesh: ctx: 16 (over z_hi, x, core), head: 8 (over z_lo, y).
Axes of the slice: x: 4, y: 4, z: 4 (z_hi: 2, z_lo: 2; z = z_hi * 2 + z_lo), core: 2. Of those that a mesh axis runs over, the one named last changes fastest.
Arguments:
- query: bfloat16 [4096, 64, 192], P('ctx', 'head'), may hold values from -12 to 12
- latents: bfloat16 [4096, 576], P('ctx'), may hold values from -4 to 4
- lat_scale: float32 [4096], P('ctx'), may hold values from 0.5 to 2
- doc_lengths: int32 [8], replicated, may hold values from 1 to 3072, 4096 in all
- w_uk: bfloat16 [64, 128, 512], P('head'), may hold values from -0.5 to 0.5
- w_uv: bfloat16 [64, 512, 128], P('head'), may hold values from -0.25 to 0.25
- w_o: bfloat16 [8192, 7168], P('head'), may hold values from -0.09375 to 0.09375
Outputs:
- attn_out: bfloat16 [4096, 7168], P('ctx', 'head')
The draws below stay inside these ranges and needn't reach their ends.
Inputs may be any that keep to these rules, and one draw needn't show every extreme that they name: `doc_lengths`: 8 lengths that sum to 4096; the longest is exactly 3072.
All inputs are finite; a program needn't handle non-finite values.
Results may differ from the reference program's by a relative error of at most 0.03.
Values may be sent and summed in bfloat16 or wider, within the bound.
A program may use at most 128 MiB of HBM per device.

```python
import math
import jax
import jax.numpy as jnp
import numpy as np
from jax import lax

D = 7168
LAT = 512
ROPE = 64
NOPE = 128
QDIM = 192
VDIM = 128
HEADS = 64
HEADS_DEV = 8
TOK_DEV = 256
TOKENS = 4096
DOCS = 8
N_CTX = 16
N_HEAD = 8


def sign_table(key):
    flips = jax.random.bernoulli(jax.random.fold_in(key, 11), 0.5, (TOKENS, ROPE))
    return jnp.where(flips, 1.0, -1.0).astype(jnp.float32)


def draw_query(key, part):
    sample = jnp.clip(jax.random.normal(jax.random.fold_in(key, 1), (TOKENS, HEADS, QDIM), jnp.float32), -4.0, 4.0)
    signs = sign_table(key)
    rope_part = 2.0 * signs[:, None, :] + 0.5 * sample[:, :, NOPE:]
    sample = jnp.concatenate([sample[:, :, :NOPE], rope_part], axis=2)
    return sample.astype(jnp.bfloat16)


def draw_latents(key, part):
    sample = jnp.clip(jax.random.normal(jax.random.fold_in(key, 4), (TOKENS, LAT + ROPE), jnp.float32), -4.0, 4.0)
    signs = sign_table(key)
    matched = jnp.roll(signs, -(TOKENS // 2), axis=0)
    rope_part = jnp.clip(2.0 * matched + 0.5 * sample[:, LAT:], -4.0, 4.0)
    sample = jnp.concatenate([sample[:, :LAT], rope_part], axis=1)
    return sample.astype(jnp.bfloat16)


def raised(entries, rng, source, target, blocks, factor):
    def block_of(axis_at):
        return (jnp.arange(entries.shape[axis_at]) // (entries.shape[axis_at] // blocks)).reshape((-1,) + (1,) * (entries.ndim - 1 - axis_at))

    first = jax.random.permutation(rng, blocks)[block_of(target)]
    other_side = (block_of(target) + blocks // 2) % blocks
    return jnp.where((block_of(source) == first) | (block_of(source) == other_side), factor * entries, entries)


def block_scale(rng, extent, split, smallest, high):
    level, own = 1.0, jax.random.fold_in(rng, 6)
    for position, shards_of in split:
        steps = jnp.exp(jax.random.uniform(jax.random.fold_in(own, position), (shards_of,), jnp.float32, smallest / len(split), high / len(split)))
        level = level * jnp.repeat(steps, extent[position] // shards_of).reshape([-1 if axis == position else 1 for axis in range(len(extent))])
    return level


def split_up(count, total, reach, lean):
    portions = [(1 << 20) // math.isqrt(rank ** lean) + 1 for rank in range(2, count + 1)]
    surplus, counts = total - reach - (count - 1), [1] * (count - 1)
    while surplus > 0:
        free = [i for i in range(count - 1) if counts[i] < reach]
        mass, left = sum([portions[i] for i in free]), surplus
        for i in free:
            extra = min(reach - counts[i], max(1, left * portions[i] // mass), surplus)
            counts[i] = counts[i] + extra
            surplus = surplus - extra
    return np.array([reach] + counts)


def ragged(own_key, number_of, total, reach, slope):
    if number_of == 2:
        one = jax.random.randint(own_key, (), max(1, total - reach), min(reach, total - 1) + 1)
        return jnp.stack([one, total - one])
    sizes = jnp.asarray(split_up(number_of, total, reach, slope), jnp.int32)
    twos = (number_of - 1) // 2
    donor, taker = sizes[1:1 + 2 * twos:2], sizes[2:2 + 2 * twos:2]
    slack = jnp.minimum(donor - 1, reach - taker)
    shifted = jax.random.randint(jax.random.fold_in(own_key, 1), (twos,), 0, 1 << 20) % (slack + 1)
    sizes = sizes.at[1:1 + 2 * twos:2].set(donor - shifted).at[2:2 + 2 * twos:2].set(taker + shifted)
    return sizes[jax.random.permutation(jax.random.fold_in(own_key, 2), number_of)]


def centred(rng, shape, deviation, most, pieces=(), kind=jnp.bfloat16):
    drawn = deviation * jax.random.normal(rng, shape, jnp.float32)
    if pieces:
        drawn = drawn * block_scale(rng, shape, pieces, -0.22, 0.18)
    return jnp.clip(drawn, -most, most).astype(kind)


def gaussian_with(key, shape, width, limit, cuts, heavy, held_as=jnp.bfloat16):
    entries = width * jax.random.normal(key, shape, jnp.float32)
    if cuts:
        entries = entries * block_scale(key, shape, cuts, -0.22, 0.18)
    return jnp.clip(raised(entries, jax.random.fold_in(key, 3), *heavy), -limit, limit).astype(held_as)


def setup_inputs(seed: int = 0) -> dict:
    splits = jax.random.split(jax.random.key(seed), 8)
    return {
        "query": draw_query(jax.random.fold_in(splits[7], 71), 0),
        "latents": draw_latents(jax.random.fold_in(splits[7], 71), 0),
        "lat_scale": jnp.clip(jnp.exp(math.log(2.0) - 1.3862944 * jax.random.uniform(splits[2], (TOKENS,), jnp.float32) ** block_scale(splits[2], (TOKENS,), ((0, 16),), -0.2, 0.2)), 0.5, 2.0),
        "doc_lengths": ragged(splits[3], DOCS, TOKENS, 3 * TOKENS // 4, 2).astype(jnp.int32),
        "w_uk": centred(splits[4], (HEADS, NOPE, LAT), NOPE ** -0.5, 0.5, ((0, 8),)),
        "w_uv": centred(splits[5], (HEADS, LAT, VDIM), LAT ** -0.5, 0.25, ((0, 8),)),
        "w_o": gaussian_with(splits[6], (HEADS * VDIM, D), (HEADS * VDIM) ** -0.5, 0.09375, ((0, 8),), (0, 1, 8, 2.0)),
    }


def segment_ids(positions, doc_ends):
    return jnp.sum((positions[:, None] >= doc_ends[None, :]).astype(jnp.int32), axis=1)


def attend(carried, query_block, query_pos, query_seg, values, key_pos, key_seg, latent_width, score_scale):
    running_max, denominator, weighted = carried
    scores = jnp.einsum("qhc,kc->qhk", query_block.astype(jnp.float32), values.astype(jnp.float32)) * score_scale
    allowed = (key_pos[None, :] <= query_pos[:, None]) & (key_seg[None, :] == query_seg[:, None])
    scores = jnp.where(allowed[:, None, :], scores, -1e30)
    new_max = jnp.maximum(running_max, jnp.max(scores, axis=2))
    weights = jnp.where(allowed[:, None, :], jnp.exp(scores - new_max[:, :, None]), 0.0)
    rescale = jnp.exp(running_max - new_max)
    denominator = denominator * rescale + jnp.sum(weights, axis=2)
    rounded = lax.optimization_barrier(weights.astype(jnp.bfloat16))
    weighted = weighted * rescale[:, :, None] + jnp.einsum(
        "qhk,kl->qhl", rounded.astype(jnp.float32), values[:, :latent_width].astype(jnp.float32))
    return new_max, denominator, weighted


def reference(query, latents, lat_scale, doc_lengths, w_uk, w_uv, w_o):
    score_scale = float(QDIM) ** -0.5
    doc_ends = jnp.cumsum(doc_lengths).astype(jnp.int32)
    query_latent = jnp.einsum("thn,hnl->thl", query[:, :, :NOPE].astype(jnp.float32),
                              w_uk.astype(jnp.float32)).astype(jnp.bfloat16)
    query_full = jnp.concatenate([query_latent, query[:, :, NOPE:]], axis=2)
    dequantized = jnp.concatenate(
        [(latents[:, :LAT].astype(jnp.float32) * lat_scale[:, None]).astype(jnp.bfloat16), latents[:, LAT:]], axis=1)

    def one_block(block_index):
        first_row = (block_index * TOK_DEV).astype(jnp.int32)
        query_block = lax.dynamic_slice_in_dim(query_full, first_row, TOK_DEV, 0)
        query_pos = first_row + jnp.arange(TOK_DEV, dtype=jnp.int32)
        query_seg = segment_ids(query_pos, doc_ends)
        initial = (jnp.full((TOK_DEV, HEADS), -1e30, jnp.float32),
                   jnp.zeros((TOK_DEV, HEADS), jnp.float32),
                   jnp.zeros((TOK_DEV, HEADS, LAT), jnp.float32))

        def key_step(key_block, carried):
            key_first = (key_block * TOK_DEV).astype(jnp.int32)
            values = lax.dynamic_slice_in_dim(dequantized, key_first, TOK_DEV, 0)
            key_pos = key_first + jnp.arange(TOK_DEV, dtype=jnp.int32)
            key_seg = segment_ids(key_pos, doc_ends)

            def update(carried_state):
                return attend(carried_state, query_block, query_pos, query_seg, values, key_pos, key_seg, LAT, score_scale)

            def unchanged(carried_state):
                return carried_state

            return lax.cond(key_block <= block_index, update, unchanged, carried)

        final_max, denominator, weighted = lax.fori_loop(0, N_CTX, key_step, initial)
        return (weighted / denominator[:, :, None]).astype(jnp.bfloat16)

    context = lax.map(one_block, jnp.arange(N_CTX, dtype=jnp.int32)).reshape(TOKENS, HEADS, LAT)
    head_out = jnp.einsum("thl,hlv->thv", context.astype(jnp.float32), w_uv.astype(jnp.float32))
    head_out = head_out.astype(jnp.bfloat16).reshape(TOKENS, HEADS * VDIM)
    group_cols = HEADS_DEV * VDIM
    total = jnp.zeros((TOKENS, D), jnp.float32)
    for group in range(N_HEAD):
        term = jnp.dot(head_out[:, group * group_cols:(group + 1) * group_cols],
                       w_o[group * group_cols:(group + 1) * group_cols], preferred_element_type=jnp.float32)
        total = total + lax.optimization_barrier(term.astype(jnp.bfloat16)).astype(jnp.float32)
    return total.astype(jnp.bfloat16)
```

```python
import functools

import jax
import jax.numpy as jnp
from jax import lax
from jax.experimental import pallas as pl
from jax.experimental.pallas import tpu as pltpu
from jax.sharding import PartitionSpec as P

LAT = 512
NOPE = 128
QDIM = 192
VDIM = 128
TOK = 256
KT = 256
PAIR = 2
NEG = -1e30
EXP_SCALE = float(QDIM) ** -0.5 * 1.4426950408889634


def attention_kernel(
    lens_ref, where_ref, q_ref, uk_ref, deq_ref, uv_ref, out_ref, qf_ref, s_ref, m_ref, l_ref, acc_ref
):
    rows = PAIR * TOK
    c = where_ref[0]
    t0 = c * TOK
    starts = []
    ends = []
    total = jnp.int32(0)
    for k in range(8):
        starts.append(total)
        total = total + lens_ref[k]
        ends.append(total)

    def start_of(t):
        first = jnp.zeros_like(t)
        for k in range(8):
            first = jnp.where(t >= ends[k], ends[k], first)
        return first

    lo_start = start_of(t0)
    hi_start = start_of(t0 + TOK - 1)
    tile_lo = lo_start // KT
    tile_mid = jnp.minimum(jnp.maximum((hi_start + KT - 1) // KT, tile_lo), c)

    for i in range(PAIR):
        q = q_ref[i]
        lat = jnp.dot(q[:, :NOPE], uk_ref[i], preferred_element_type=jnp.float32)
        qf_ref[i * TOK : (i + 1) * TOK, :LAT] = lat.astype(jnp.bfloat16)
        qf_ref[i * TOK : (i + 1) * TOK, LAT:] = q[:, NOPE:]

    m_ref[...] = jnp.full_like(m_ref, NEG)

    def scores(j):
        keys = deq_ref[pl.ds(pl.multiple_of(j * KT, KT), KT), :]
        return lax.dot_general(
            qf_ref[...], keys, (((1,), (1,)), ((), ())), preferred_element_type=jnp.float32
        )

    def put(j, s):
        s_ref[j] = s
        m_ref[...] = jnp.maximum(m_ref[...], jnp.maximum(s[:, :128], s[:, 128:]))

    def masked(j, carry):
        s = scores(j)
        qpos = t0 + lax.broadcasted_iota(jnp.int32, (rows, 1), 0) % TOK
        first = start_of(qpos)
        kpos = j * KT + lax.broadcasted_iota(jnp.int32, (rows, KT), 1)
        put(j, jnp.where((kpos >= first) & (kpos <= qpos), s, NEG))
        return carry

    def plain(j, carry):
        put(j, scores(j))
        return carry

    lax.fori_loop(tile_lo, tile_mid, masked, 0)
    lax.fori_loop(tile_mid, c, plain, 0)
    masked(c, 0)

    pair_lo = tile_lo // 2
    pair_hi = c // 2

    @pl.when(tile_lo % 2 == 1)
    def _():
        s_ref[tile_lo - 1] = jnp.full((rows, KT), NEG, jnp.float32)

    @pl.when(c % 2 == 0)
    def _():
        s_ref[c + 1] = jnp.full((rows, KT), NEG, jnp.float32)

    m = jnp.max(m_ref[...], axis=1, keepdims=True)
    m_ref[...] = jnp.broadcast_to(m, m_ref.shape)
    l_ref[...] = jnp.zeros_like(l_ref)
    acc_ref[...] = jnp.zeros_like(acc_ref)

    def weigh(j, carry):
        top = m_ref[...]
        parts = []
        total = l_ref[...]
        for half in range(2):
            s = s_ref[2 * j + half]
            for lane in range(0, KT, 128):
                p = jnp.exp2((s[:, lane : lane + 128] - top) * EXP_SCALE)
                total = total + p
                parts.append(p.astype(jnp.bfloat16))
        l_ref[...] = total
        p = jnp.concatenate(parts, axis=1)
        values = deq_ref[pl.ds(pl.multiple_of(j * 2 * KT, 2 * KT), 2 * KT), :LAT]
        acc_ref[...] += jnp.dot(p, values, preferred_element_type=jnp.float32)
        return carry

    lax.fori_loop(pair_lo, pair_hi + 1, weigh, 0)
    denominator = jnp.sum(l_ref[...], axis=1, keepdims=True)
    context = (acc_ref[...] / denominator).astype(jnp.bfloat16)
    for i in range(PAIR):
        head = jnp.dot(
            context[i * TOK : (i + 1) * TOK], uv_ref[i], preferred_element_type=jnp.float32
        )
        out_ref[:, i * VDIM : (i + 1) * VDIM] = head.astype(jnp.bfloat16)


def attention(doc_lengths, ctx_index, query, w_uk, deq, w_uv):
    heads = query.shape[0]
    keys = deq.shape[0]
    rows = PAIR * TOK
    return pl.pallas_call(
        attention_kernel,
        out_shape=jax.ShapeDtypeStruct((TOK, heads * VDIM), jnp.bfloat16),
        grid_spec=pltpu.PrefetchScalarGridSpec(
            num_scalar_prefetch=2,
            grid=(heads // PAIR,),
            in_specs=[
                pl.BlockSpec((PAIR, TOK, QDIM), lambda i, a, b: (i, 0, 0)),
                pl.BlockSpec((PAIR, NOPE, LAT), lambda i, a, b: (i, 0, 0)),
                pl.BlockSpec((keys, deq.shape[1]), lambda i, a, b: (0, 0)),
                pl.BlockSpec((PAIR, LAT, VDIM), lambda i, a, b: (i, 0, 0)),
            ],
            out_specs=pl.BlockSpec((TOK, PAIR * VDIM), lambda i, a, b: (0, i)),
            scratch_shapes=[
                pltpu.VMEM((rows, deq.shape[1]), jnp.bfloat16),
                pltpu.VMEM((keys // KT, rows, KT), jnp.float32),
                pltpu.VMEM((rows, 128), jnp.float32),
                pltpu.VMEM((rows, 128), jnp.float32),
                pltpu.VMEM((rows, LAT), jnp.float32),
            ],
        ),
        compiler_params=pltpu.CompilerParams(vmem_limit_bytes=40 << 20),
        name="attention",
    )(doc_lengths, ctx_index, query, w_uk, deq, w_uv)


def shards(query, latents, lat_scale, doc_lengths, w_uk, w_uv, w_o):
    ctx_index = lax.axis_index("ctx").astype(jnp.int32).reshape(1)
    scaled = (latents[:, :LAT].astype(jnp.float32) * lat_scale[:, None]).astype(jnp.bfloat16)
    deq = jnp.concatenate([scaled, latents[:, LAT:]], axis=1)
    deq = lax.all_gather(deq, "ctx", axis=0, tiled=True)
    by_head = jnp.transpose(query, (1, 0, 2))
    head_out = attention(doc_lengths, ctx_index, by_head, w_uk, deq, w_uv)
    partial_value = jnp.dot(head_out, w_o, preferred_element_type=jnp.float32)
    return lax.psum_scatter(
        partial_value.astype(jnp.bfloat16), "head", scatter_dimension=1, tiled=True
    )


def solution(mesh):
    placed = (
        P("ctx", "head", None),
        P("ctx", None),
        P("ctx"),
        P(),
        P("head", None, None),
        P("head", None, None),
        P("head", None),
    )
    return jax.shard_map(
        shards, mesh=mesh, in_specs=placed, out_specs=P("ctx", "head"), check_vma=False
    )
```

```python
import jax
import jax.numpy as jnp
from jax import lax
from jax.experimental import pallas as pl
from jax.experimental.pallas import tpu as pltpu
from jax.sharding import PartitionSpec as P

LAT = 512
NOPE = 128
QDIM = 192
VDIM = 128
TOK = 256
KT = 256
PAIR = 2
NEG = -1e30
MESH = pl.DeviceIdType.MESH
EXP_SCALE = float(QDIM) ** -0.5 * 1.4426950408889634


def attention_kernel(
    lens_ref, where_ref, q_ref, uk_ref, deq_ref, uv_ref, out_ref, qf_ref, s_ref, m_ref, l_ref, acc_ref
):
    rows = PAIR * TOK
    c = where_ref[0]
    t0 = c * TOK
    starts = []
    ends = []
    total = jnp.int32(0)
    for k in range(8):
        starts.append(total)
        total = total + lens_ref[k]
        ends.append(total)

    def start_of(t):
        first = jnp.zeros_like(t)
        for k in range(8):
            first = jnp.where(t >= ends[k], ends[k], first)
        return first

    lo_start = start_of(t0)
    hi_start = start_of(t0 + TOK - 1)
    tile_lo = lo_start // KT
    tile_mid = jnp.minimum(jnp.maximum((hi_start + KT - 1) // KT, tile_lo), c)

    for i in range(PAIR):
        q = q_ref[i]
        lat = jnp.dot(q[:, :NOPE], uk_ref[i], preferred_element_type=jnp.float32)
        qf_ref[i * TOK : (i + 1) * TOK, :LAT] = lat.astype(jnp.bfloat16)
        qf_ref[i * TOK : (i + 1) * TOK, LAT:] = q[:, NOPE:]

    m_ref[...] = jnp.full_like(m_ref, NEG)

    def scores(j):
        keys = deq_ref[pl.ds(pl.multiple_of(j * KT, KT), KT), :]
        return lax.dot_general(
            qf_ref[...], keys, (((1,), (1,)), ((), ())), preferred_element_type=jnp.float32
        )

    def put(j, s):
        s_ref[j] = s
        m_ref[...] = jnp.maximum(m_ref[...], jnp.maximum(s[:, :128], s[:, 128:]))

    def masked(j, carry):
        s = scores(j)
        qpos = t0 + lax.broadcasted_iota(jnp.int32, (rows, 1), 0) % TOK
        first = start_of(qpos)
        kpos = j * KT + lax.broadcasted_iota(jnp.int32, (rows, KT), 1)
        put(j, jnp.where((kpos >= first) & (kpos <= qpos), s, NEG))
        return carry

    def plain(j, carry):
        put(j, scores(j))
        return carry

    lax.fori_loop(tile_lo, tile_mid, masked, 0)
    lax.fori_loop(tile_mid, c, plain, 0)
    masked(c, 0)

    pair_lo = tile_lo // 2
    pair_hi = c // 2

    @pl.when(tile_lo % 2 == 1)
    def _():
        s_ref[tile_lo - 1] = jnp.full((rows, KT), NEG, jnp.float32)

    @pl.when(c % 2 == 0)
    def _():
        s_ref[c + 1] = jnp.full((rows, KT), NEG, jnp.float32)

    m = jnp.max(m_ref[...], axis=1, keepdims=True)
    m_ref[...] = jnp.broadcast_to(m, m_ref.shape)
    l_ref[...] = jnp.zeros_like(l_ref)
    acc_ref[...] = jnp.zeros_like(acc_ref)

    def weigh(j, carry):
        top = m_ref[...]
        parts = []
        total = l_ref[...]
        for half in range(2):
            s = s_ref[2 * j + half]
            for lane in range(0, KT, 128):
                p = jnp.exp2((s[:, lane : lane + 128] - top) * EXP_SCALE)
                total = total + p
                parts.append(p.astype(jnp.bfloat16))
        l_ref[...] = total
        p = jnp.concatenate(parts, axis=1)
        values = deq_ref[pl.ds(pl.multiple_of(j * 2 * KT, 2 * KT), 2 * KT), :LAT]
        acc_ref[...] += jnp.dot(p, values, preferred_element_type=jnp.float32)
        return carry

    lax.fori_loop(pair_lo, pair_hi + 1, weigh, 0)
    denominator = jnp.sum(l_ref[...], axis=1, keepdims=True)
    context = (acc_ref[...] / denominator).astype(jnp.bfloat16)
    for i in range(PAIR):
        head = jnp.dot(
            context[i * TOK : (i + 1) * TOK], uv_ref[i], preferred_element_type=jnp.float32
        )
        out_ref[:, i * VDIM : (i + 1) * VDIM] = head.astype(jnp.bfloat16)


def attention(doc_lengths, ctx_index, query, w_uk, deq, w_uv):
    heads = query.shape[0]
    keys = deq.shape[0]
    rows = PAIR * TOK
    return pl.pallas_call(
        attention_kernel,
        out_shape=jax.ShapeDtypeStruct((TOK, heads * VDIM), jnp.bfloat16),
        grid_spec=pltpu.PrefetchScalarGridSpec(
            num_scalar_prefetch=2,
            grid=(heads // PAIR,),
            in_specs=[
                pl.BlockSpec((PAIR, TOK, QDIM), lambda i, a, b: (i, 0, 0)),
                pl.BlockSpec((PAIR, NOPE, LAT), lambda i, a, b: (i, 0, 0)),
                pl.BlockSpec((keys, deq.shape[1]), lambda i, a, b: (0, 0)),
                pl.BlockSpec((PAIR, LAT, VDIM), lambda i, a, b: (i, 0, 0)),
            ],
            out_specs=pl.BlockSpec((TOK, PAIR * VDIM), lambda i, a, b: (0, i)),
            scratch_shapes=[
                pltpu.VMEM((rows, deq.shape[1]), jnp.bfloat16),
                pltpu.VMEM((keys // KT, rows, KT), jnp.float32),
                pltpu.VMEM((rows, 128), jnp.float32),
                pltpu.VMEM((rows, 128), jnp.float32),
                pltpu.VMEM((rows, LAT), jnp.float32),
            ],
        ),
        compiler_params=pltpu.CompilerParams(vmem_limit_bytes=40 << 20),
        name="attention",
    )(doc_lengths, ctx_index, query, w_uk, deq, w_uv)


def reduce_kernel(
    x_ref, w_ref, out_ref, wbuf, own, zrecv, y1recv, y2recv, ysecond1, ysecond2, zlast,
    wsem, zsend, zgot, y1send, y1got, y2send, y2got, s1send, s1got, s2send, s2got, lsend, lgot,
):
    cols = out_ref.shape[1]
    half = out_ref.shape[0] // 2
    quarter = half // 2
    me = lax.axis_index("head")
    y = lax.rem(me, 4)
    z = me // 4
    up = z * 4 + lax.rem(y + 1, 4)
    down = z * 4 + lax.rem(y + 3, 4)
    across = (1 - z) * 4 + y
    blocks = ((2, 0), (2, 1), (1, 0), (3, 0), (1, 1), (3, 1), (0, 0), (0, 1))
    slot = {key: k for k, key in enumerate(blocks)}
    first = pl.ds(0, half)
    second = pl.ds(half, half)

    def fetch(k):
        shift, mine = blocks[k]
        plane = z if mine else 1 - z
        start = pl.multiple_of((plane * 4 + lax.rem(y + shift, 4)) * cols, 128)
        return pltpu.make_async_copy(w_ref.at[:, pl.ds(start, cols)], wbuf.at[k], wsem.at[k])

    def send(src, dst, ssem, rsem, target):
        return pltpu.make_async_remote_copy(
            src_ref=src, dst_ref=dst, send_sem=ssem, recv_sem=rsem,
            device_id={"head": target}, device_id_type=MESH,
        )

    for k in range(8):
        fetch(k).start()
    barrier = pltpu.get_barrier_semaphore()
    for target in (up, down, across):
        pl.semaphore_signal(barrier, inc=1, device_id={"head": target}, device_id_type=MESH)
    pl.semaphore_wait(barrier, 3)

    pending = []

    def go(copy):
        copy.start()
        pending.append(copy)

    def across_copy(i, k):
        return send(own.at[k, first], zrecv.at[i], zsend.at[i], zgot.at[i], across)

    def step1(k, base, buf, ssem, rsem, i):
        go(send(own.at[k, pl.ds(base, quarter)], buf.at[i], ssem.at[i], rsem.at[i], up))
        go(
            send(
                own.at[k, pl.ds(base + quarter, quarter)],
                buf.at[i + 1], ssem.at[i + 1], rsem.at[i + 1], down,
            )
        )

    across_order = (2, 1, 3, 0)
    across_copies = {}

    def compute(k):
        fetch(k).wait()
        own[k] = jnp.dot(x_ref[...], wbuf[k], preferred_element_type=jnp.float32).astype(
            jnp.bfloat16
        )
        shift, mine = blocks[k]
        if not mine:
            i = across_order.index(shift)
            across_copies[i] = across_copy(i, k)
            go(across_copies[i])
        if shift == 2:
            step1(k, half, y1recv, y1send, y1got, 2 * mine)

    def add_rows(k, rows, *terms):
        total = own[k, rows].astype(jnp.float32)
        for term in terms:
            total = total + term.astype(jnp.float32)
        return total

    copies = {}

    def y_first_step2(mine):
        for side, (shift, target, offset) in enumerate(((1, up, 0), (3, down, quarter))):
            k = slot[(shift, mine)]
            i = 2 * mine + side
            rows = pl.ds(half + offset, quarter)
            send(
                own.at[0, pl.ds(0, quarter)], y1recv.at[i], y1send.at[i], y1got.at[i], target
            ).wait_recv()
            own[k, rows] = add_rows(k, rows, y1recv[i]).astype(jnp.bfloat16)
            go(send(own.at[k, second], y2recv.at[i], y2send.at[i], y2got.at[i], target))

    def got(buf, i, ssem, rsem, rows):
        send(own.at[0, pl.ds(0, rows)], buf.at[i], ssem.at[i], rsem.at[i], across).wait_recv()

    for k in range(6):
        compute(k)
    y_first_step2(0)
    for k in range(6, 8):
        compute(k)
    y_first_step2(1)

    got(zrecv, 0, zsend, zgot, half)
    k = slot[(2, 1)]
    own[k, first] = add_rows(k, first, zrecv[0]).astype(jnp.bfloat16)
    step1(k, 0, ysecond1, s1send, s1got, 0)

    got(y2recv, 0, y2send, y2got, half)
    got(y2recv, 1, y2send, y2got, half)
    k = slot[(0, 0)]
    own[k, second] = add_rows(k, second, y2recv[0], y2recv[1]).astype(jnp.bfloat16)
    go(send(own.at[k, second], zlast.at[0], lsend.at[0], lgot.at[0], across))

    for side, (shift, target, offset) in enumerate(((1, up, 0), (3, down, quarter))):
        k = slot[(shift, 1)]
        got(zrecv, 1 + side, zsend, zgot, half)
        got(ysecond1, side, s1send, s1got, quarter)
        own[k, first] = add_rows(k, first, zrecv[1 + side]).astype(jnp.bfloat16)
        rows = pl.ds(offset, quarter)
        own[k, rows] = add_rows(k, rows, ysecond1[side]).astype(jnp.bfloat16)
        go(send(own.at[k, first], ysecond2.at[side], s2send.at[side], s2got.at[side], target))

    k = slot[(0, 1)]
    got(y2recv, 2, y2send, y2got, half)
    got(y2recv, 3, y2send, y2got, half)
    got(zlast, 0, lsend, lgot, half)
    out_ref[second] = add_rows(k, second, y2recv[2], y2recv[3], zlast[0]).astype(jnp.bfloat16)
    got(zrecv, 3, zsend, zgot, half)
    got(ysecond2, 0, s2send, s2got, half)
    got(ysecond2, 1, s2send, s2got, half)
    out_ref[first] = add_rows(k, first, zrecv[3], ysecond2[0], ysecond2[1]).astype(jnp.bfloat16)
    for copy in pending:
        copy.wait_send()


def project_and_reduce(head_out, w_o):
    rows, inner = head_out.shape
    cols = w_o.shape[1] // 8
    half = rows // 2
    dma = pltpu.SemaphoreType.DMA
    return pl.pallas_call(
        reduce_kernel,
        out_shape=jax.ShapeDtypeStruct((rows, cols), jnp.bfloat16),
        in_specs=[pl.BlockSpec(memory_space=pltpu.VMEM), pl.BlockSpec(memory_space=pl.ANY)],
        out_specs=pl.BlockSpec(memory_space=pltpu.VMEM),
        scratch_shapes=[
            pltpu.VMEM((8, inner, cols), jnp.bfloat16),
            pltpu.VMEM((8, rows, cols), jnp.bfloat16),
            pltpu.VMEM((4, half, cols), jnp.bfloat16),
            pltpu.VMEM((4, half // 2, cols), jnp.bfloat16),
            pltpu.VMEM((4, half, cols), jnp.bfloat16),
            pltpu.VMEM((2, half // 2, cols), jnp.bfloat16),
            pltpu.VMEM((2, half, cols), jnp.bfloat16),
            pltpu.VMEM((1, half, cols), jnp.bfloat16),
            dma((8,)),
            dma((4,)), dma((4,)),
            dma((4,)), dma((4,)),
            dma((4,)), dma((4,)),
            dma((2,)), dma((2,)),
            dma((2,)), dma((2,)),
            dma((1,)), dma((1,)),
        ],
        compiler_params=pltpu.CompilerParams(
            collective_id=0, has_side_effects=True, vmem_limit_bytes=40 << 20
        ),
        name="project_and_reduce",
    )(head_out, w_o)


def shards(query, latents, lat_scale, doc_lengths, w_uk, w_uv, w_o):
    ctx_index = lax.axis_index("ctx").astype(jnp.int32).reshape(1)
    scaled = (latents[:, :LAT].astype(jnp.float32) * lat_scale[:, None]).astype(jnp.bfloat16)
    deq = jnp.concatenate([scaled, latents[:, LAT:]], axis=1)
    deq = lax.all_gather(deq, "ctx", axis=0, tiled=True)
    by_head = jnp.transpose(query, (1, 0, 2))
    head_out = attention(doc_lengths, ctx_index, by_head, w_uk, deq, w_uv)
    return project_and_reduce(head_out, w_o)


def solution(mesh):
    placed = (
        P("ctx", "head", None),
        P("ctx", None),
        P("ctx"),
        P(),
        P("head", None, None),
        P("head", None, None),
        P("head", None),
    )
    return jax.shard_map(
        shards, mesh=mesh, in_specs=placed, out_specs=P("ctx", "head"), check_vma=False
    )
```

```python
import jax
import jax.numpy as jnp
from jax import lax
from jax.experimental import pallas as pl
from jax.experimental.pallas import tpu as pltpu
from jax.sharding import PartitionSpec as P

LAT = 512
NOPE = 128
QDIM = 192
VDIM = 128
TOK = 256
KT = 256
GROUP = 4
PER = 4
NEG = -1e30
MESH = pl.DeviceIdType.MESH
EXP_SCALE = float(QDIM) ** -0.5 * 1.4426950408889634


def attention_kernel(lens_ref, qf_ref, keys_ref, uv_ref, out_ref, s_ref, m_ref, l_ref, acc_ref):
    rows = m_ref.shape[0]
    group = rows // TOK
    ctx = lax.axis_index("ctx")
    t0 = ctx * TOK
    ends = []
    total = jnp.int32(0)
    for k in range(lens_ref.shape[0]):
        total = total + lens_ref[k]
        ends.append(total)

    def start_of(t):
        first = jnp.zeros_like(t)
        for end in ends:
            first = jnp.where(t >= end, end, first)
        return first

    tile_lo = start_of(t0) // KT
    tile_mid = jnp.clip((start_of(t0 + TOK - 1) + KT - 1) // KT, tile_lo, ctx)
    chunk_lo = tile_lo // PER
    chunk_hi = ctx // PER

    def one_group(g, carry):
        base = pl.multiple_of(g * rows, rows)
        m_ref[...] = jnp.full_like(m_ref, NEG)

        def scores(j):
            keys = keys_ref[pl.ds(pl.multiple_of(j * KT, KT), KT), :]
            return lax.dot_general(
                qf_ref[pl.ds(base, rows), :],
                keys,
                (((1,), (1,)), ((), ())),
                preferred_element_type=jnp.float32,
            )

        def put(j, s):
            s_ref[j] = s
            m_ref[...] = jnp.maximum(m_ref[...], jnp.maximum(s[:, :128], s[:, 128:]))

        def masked(j, carry):
            s = scores(j)
            qpos = t0 + lax.broadcasted_iota(jnp.int32, (rows, 1), 0) % TOK
            first = start_of(qpos)
            kpos = j * KT + lax.broadcasted_iota(jnp.int32, (rows, KT), 1)
            put(j, jnp.where((kpos >= first) & (kpos <= qpos), s, NEG))
            return carry

        def plain(j, carry):
            put(j, scores(j))
            return carry

        def clear(j, carry):
            s_ref[j] = jnp.full((rows, KT), NEG, jnp.float32)
            return carry

        lax.fori_loop(chunk_lo * PER, tile_lo, clear, 0)
        lax.fori_loop(tile_lo, tile_mid, masked, 0)
        lax.fori_loop(tile_mid, ctx, plain, 0)
        masked(ctx, 0)
        lax.fori_loop(ctx + 1, (chunk_hi + 1) * PER, clear, 0)

        m = jnp.max(m_ref[...], axis=1, keepdims=True)
        m_ref[...] = jnp.broadcast_to(m, m_ref.shape)
        l_ref[...] = jnp.zeros_like(l_ref)
        acc_ref[...] = jnp.zeros_like(acc_ref)

        def weigh(j, carry):
            top = m_ref[...]
            parts = []
            total = l_ref[...]
            for tile in range(PER):
                s = s_ref[PER * j + tile]
                for lane in range(0, KT, 128):
                    p = jnp.exp2((s[:, lane : lane + 128] - top) * EXP_SCALE)
                    total = total + p
                    parts.append(p.astype(jnp.bfloat16))
            l_ref[...] = total
            p = jnp.concatenate(parts, axis=1)
            chunk = PER * KT
            values = keys_ref[pl.ds(pl.multiple_of(j * chunk, chunk), chunk), :LAT]
            acc_ref[...] += jnp.dot(p, values, preferred_element_type=jnp.float32)
            return carry

        lax.fori_loop(chunk_lo, chunk_hi + 1, weigh, 0)
        denominator = jnp.sum(l_ref[...], axis=1, keepdims=True)
        context = (acc_ref[...] / denominator).astype(jnp.bfloat16)
        for i in range(group):
            h = g * group + i
            head = jnp.dot(
                context[i * TOK : (i + 1) * TOK], uv_ref[h], preferred_element_type=jnp.float32
            )
            out_ref[:, pl.ds(pl.multiple_of(h * VDIM, VDIM), VDIM)] = head.astype(jnp.bfloat16)
        return carry

    lax.fori_loop(0, qf_ref.shape[0] // rows, one_group, 0)


def attention(doc_lengths, query_full, keys, w_uv):
    heads = w_uv.shape[0]
    length = keys.shape[0]
    rows = GROUP * TOK
    vmem = pl.BlockSpec(memory_space=pltpu.VMEM)
    return pl.pallas_call(
        attention_kernel,
        out_shape=jax.ShapeDtypeStruct((TOK, heads * VDIM), jnp.bfloat16),
        in_specs=[pl.BlockSpec(memory_space=pltpu.SMEM), vmem, vmem, vmem],
        out_specs=vmem,
        scratch_shapes=[
            pltpu.VMEM((length // KT, rows, KT), jnp.float32),
            pltpu.VMEM((rows, 128), jnp.float32),
            pltpu.VMEM((rows, 128), jnp.float32),
            pltpu.VMEM((rows, LAT), jnp.float32),
        ],
        compiler_params=pltpu.CompilerParams(vmem_limit_bytes=44 << 20),
        name="attention",
    )(doc_lengths, query_full, keys, w_uv)


def reduce_kernel(
    x_ref, w_ref, out_ref, wbuf, own, zrecv, y1recv, y2recv, ysecond1, ysecond2, zlast,
    wsem, zsend, zgot, y1send, y1got, y2send, y2got, s1send, s1got, s2send, s2got, lsend, lgot,
):
    cols = out_ref.shape[1]
    half = out_ref.shape[0] // 2
    quarter = half // 2
    me = lax.axis_index("head")
    y = lax.rem(me, 4)
    z = me // 4
    up = z * 4 + lax.rem(y + 1, 4)
    down = z * 4 + lax.rem(y + 3, 4)
    across = (1 - z) * 4 + y
    blocks = ((2, 0), (2, 1), (1, 0), (3, 0), (1, 1), (3, 1), (0, 0), (0, 1))
    slot = {key: k for k, key in enumerate(blocks)}
    first = pl.ds(0, half)
    second = pl.ds(half, half)

    def fetch(k):
        shift, mine = blocks[k]
        plane = z if mine else 1 - z
        start = pl.multiple_of((plane * 4 + lax.rem(y + shift, 4)) * cols, 128)
        return pltpu.make_async_copy(w_ref.at[:, pl.ds(start, cols)], wbuf.at[k], wsem.at[k])

    def send(src, dst, ssem, rsem, target):
        return pltpu.make_async_remote_copy(
            src_ref=src, dst_ref=dst, send_sem=ssem, recv_sem=rsem,
            device_id={"head": target}, device_id_type=MESH,
        )

    for k in range(8):
        fetch(k).start()
    barrier = pltpu.get_barrier_semaphore()
    for target in (up, down, across):
        pl.semaphore_signal(barrier, inc=1, device_id={"head": target}, device_id_type=MESH)
    pl.semaphore_wait(barrier, 3)

    pending = []

    def go(copy):
        copy.start()
        pending.append(copy)

    def across_copy(i, k):
        return send(own.at[k, first], zrecv.at[i], zsend.at[i], zgot.at[i], across)

    def step1(k, base, buf, ssem, rsem, i):
        go(send(own.at[k, pl.ds(base, quarter)], buf.at[i], ssem.at[i], rsem.at[i], up))
        go(
            send(
                own.at[k, pl.ds(base + quarter, quarter)],
                buf.at[i + 1], ssem.at[i + 1], rsem.at[i + 1], down,
            )
        )

    across_order = (2, 1, 3, 0)
    across_copies = {}

    def compute(k):
        fetch(k).wait()
        own[k] = jnp.dot(x_ref[...], wbuf[k], preferred_element_type=jnp.float32).astype(
            jnp.bfloat16
        )
        shift, mine = blocks[k]
        if not mine:
            i = across_order.index(shift)
            across_copies[i] = across_copy(i, k)
            go(across_copies[i])
        if shift == 2:
            step1(k, half, y1recv, y1send, y1got, 2 * mine)

    def add_rows(k, rows, *terms):
        total = own[k, rows].astype(jnp.float32)
        for term in terms:
            total = total + term.astype(jnp.float32)
        return total

    copies = {}

    def y_first_step2(mine):
        for side, (shift, target, offset) in enumerate(((1, up, 0), (3, down, quarter))):
            k = slot[(shift, mine)]
            i = 2 * mine + side
            rows = pl.ds(half + offset, quarter)
            send(
                own.at[0, pl.ds(0, quarter)], y1recv.at[i], y1send.at[i], y1got.at[i], target
            ).wait_recv()
            own[k, rows] = add_rows(k, rows, y1recv[i]).astype(jnp.bfloat16)
            go(send(own.at[k, second], y2recv.at[i], y2send.at[i], y2got.at[i], target))

    def got(buf, i, ssem, rsem, rows):
        send(own.at[0, pl.ds(0, rows)], buf.at[i], ssem.at[i], rsem.at[i], across).wait_recv()

    for k in range(6):
        compute(k)
    y_first_step2(0)
    for k in range(6, 8):
        compute(k)
    y_first_step2(1)

    got(zrecv, 0, zsend, zgot, half)
    k = slot[(2, 1)]
    own[k, first] = add_rows(k, first, zrecv[0]).astype(jnp.bfloat16)
    step1(k, 0, ysecond1, s1send, s1got, 0)

    got(y2recv, 0, y2send, y2got, half)
    got(y2recv, 1, y2send, y2got, half)
    k = slot[(0, 0)]
    own[k, second] = add_rows(k, second, y2recv[0], y2recv[1]).astype(jnp.bfloat16)
    go(send(own.at[k, second], zlast.at[0], lsend.at[0], lgot.at[0], across))

    for side, (shift, target, offset) in enumerate(((1, up, 0), (3, down, quarter))):
        k = slot[(shift, 1)]
        got(zrecv, 1 + side, zsend, zgot, half)
        got(ysecond1, side, s1send, s1got, quarter)
        own[k, first] = add_rows(k, first, zrecv[1 + side]).astype(jnp.bfloat16)
        rows = pl.ds(offset, quarter)
        own[k, rows] = add_rows(k, rows, ysecond1[side]).astype(jnp.bfloat16)
        go(send(own.at[k, first], ysecond2.at[side], s2send.at[side], s2got.at[side], target))

    k = slot[(0, 1)]
    got(y2recv, 2, y2send, y2got, half)
    got(y2recv, 3, y2send, y2got, half)
    got(zlast, 0, lsend, lgot, half)
    out_ref[second] = add_rows(k, second, y2recv[2], y2recv[3], zlast[0]).astype(jnp.bfloat16)
    got(zrecv, 3, zsend, zgot, half)
    got(ysecond2, 0, s2send, s2got, half)
    got(ysecond2, 1, s2send, s2got, half)
    out_ref[first] = add_rows(k, first, zrecv[3], ysecond2[0], ysecond2[1]).astype(jnp.bfloat16)
    for copy in pending:
        copy.wait_send()


def project_and_reduce(head_out, w_o):
    rows, inner = head_out.shape
    cols = w_o.shape[1] // 8
    half = rows // 2
    dma = pltpu.SemaphoreType.DMA
    return pl.pallas_call(
        reduce_kernel,
        out_shape=jax.ShapeDtypeStruct((rows, cols), jnp.bfloat16),
        in_specs=[pl.BlockSpec(memory_space=pltpu.VMEM), pl.BlockSpec(memory_space=pl.ANY)],
        out_specs=pl.BlockSpec(memory_space=pltpu.VMEM),
        scratch_shapes=[
            pltpu.VMEM((8, inner, cols), jnp.bfloat16),
            pltpu.VMEM((8, rows, cols), jnp.bfloat16),
            pltpu.VMEM((4, half, cols), jnp.bfloat16),
            pltpu.VMEM((4, half // 2, cols), jnp.bfloat16),
            pltpu.VMEM((4, half, cols), jnp.bfloat16),
            pltpu.VMEM((2, half // 2, cols), jnp.bfloat16),
            pltpu.VMEM((2, half, cols), jnp.bfloat16),
            pltpu.VMEM((1, half, cols), jnp.bfloat16),
            dma((8,)),
            dma((4,)), dma((4,)),
            dma((4,)), dma((4,)),
            dma((4,)), dma((4,)),
            dma((2,)), dma((2,)),
            dma((2,)), dma((2,)),
            dma((1,)), dma((1,)),
        ],
        compiler_params=pltpu.CompilerParams(
            collective_id=0, has_side_effects=True, vmem_limit_bytes=40 << 20
        ),
        name="project_and_reduce",
    )(head_out, w_o)


def gather_kernel(
    q_ref, latents_ref, scale_ref, uk_ref, keys_ref, qf_ref,
    zsend, zgot, x1send, x1got, x2send, x2got, y1send, y1got, y2send, y2got, csend, cgot,
):
    rows = latents_ref.shape[0]
    direct = rows // 2
    part = (rows - direct) // 4
    ctx = lax.axis_index("ctx")
    head = lax.axis_index("head")
    core = lax.rem(ctx, 2)
    x = lax.rem(ctx // 2, 4)
    hi = ctx // 8
    y = lax.rem(head, 4)
    lo = head // 4
    x_up, x_down, x_far = lax.rem(x + 1, 4), lax.rem(x + 3, 4), lax.rem(x + 2, 4)
    y_up, y_down, y_far = lax.rem(y + 1, 4), lax.rem(y + 3, 4), lax.rem(y + 2, 4)
    planes = (hi * 4, (1 - hi) * 4)

    def place(a, b, c, d, e):
        return {"ctx": a * 8 + b * 2 + c, "head": d * 4 + e}

    to_x = (place(hi, x_up, core, lo, y), place(hi, x_down, core, lo, y))
    to_y = (place(hi, x, core, lo, y_up), place(hi, x, core, lo, y_down))
    to_z = place(1 - hi, x, core, 1 - lo, y)
    to_core = place(hi, x, 1 - core, lo, y)

    def strip(index):
        return pl.ds(pl.multiple_of(direct + index * part, 16), part)

    def strip_half(index, which):
        return pl.ds(pl.multiple_of(direct + index * part + which * (part // 2), 16), part // 2)

    sets = (strip(y), pl.ds(0, direct))
    set_halves = (
        (strip_half(y, 0), strip_half(y, 1)),
        (pl.ds(0, direct // 2), pl.ds(direct // 2, direct // 2)),
    )

    def copy(src, dst, ssem, rsem, target):
        return pltpu.make_async_remote_copy(
            src_ref=src, dst_ref=dst, send_sem=ssem, recv_sem=rsem,
            device_id=target, device_id_type=MESH,
        )

    pending = []

    def go(ref, ssem, rsem, target):
        one = copy(ref, ref, ssem, rsem, target)
        one.start()
        pending.append(one)

    def got(ref, ssem, rsem):
        copy(ref, ref, ssem, rsem, to_core).wait_recv()

    barrier = pltpu.get_barrier_semaphore()
    for target in (*to_x, *to_y, to_z, to_core):
        pl.semaphore_signal(barrier, inc=1, device_id=target, device_id_type=MESH)

    eye = lax.broadcasted_iota(jnp.int32, (rows, rows), 0) == lax.broadcasted_iota(
        jnp.int32, (rows, rows), 1
    )
    column = jnp.sum(jnp.where(eye, scale_ref[...], 0.0), axis=1, keepdims=True)
    mine = planes[0] + x
    latent = latents_ref[...]
    keys_ref[mine, core, :, :LAT] = (latent[:, :LAT].astype(jnp.float32) * column).astype(
        jnp.bfloat16
    )
    keys_ref[mine, core, :, LAT:] = latent[:, LAT:]

    pl.semaphore_wait(barrier, 6)

    def x_step1(plane, s):
        ref = keys_ref.at[planes[plane] + x, core, sets[s]]
        for d in range(2):
            i = (plane * 2 + s) * 2 + d
            go(ref, x1send.at[i], x1got.at[i], to_x[d])

    for s in range(2):
        ref = keys_ref.at[mine, core, sets[s]]
        go(ref, zsend.at[s], zgot.at[s], to_z)
        x_step1(0, s)
    for s, part_rows in enumerate((pl.ds(direct, rows - direct), pl.ds(0, direct))):
        i = s * 4
        go(keys_ref.at[mine, core, part_rows], csend.at[i], cgot.at[i], to_core)

    for h in range(q_ref.shape[0]):
        q = q_ref[h]
        lat = jnp.dot(q[:, :NOPE], uk_ref[h], preferred_element_type=jnp.float32)
        qf_ref[h, :, :LAT] = lat.astype(jnp.bfloat16)
        qf_ref[h, :, LAT:] = q[:, NOPE:]

    def x_step2(plane, s):
        for d, source in enumerate((x_down, x_up)):
            i = (plane * 2 + s) * 2 + d
            got(keys_ref.at[planes[plane] + source, core, sets[s]], x1send.at[i], x1got.at[i])
            ref = keys_ref.at[planes[plane] + source, core, set_halves[s][d]]
            go(ref, x2send.at[i], x2got.at[i], to_x[d])

    def x_finish(plane, s):
        for d in range(2):
            i = (plane * 2 + s) * 2 + d
            ref = keys_ref.at[planes[plane] + x_far, core, set_halves[s][d]]
            got(ref, x2send.at[i], x2got.at[i])

    around = (x, x_up, x_far, x_down)

    def block(plane, r):
        return planes[plane] + around[r]

    onward = {(0, 1): 0, (0, 2): 0, (0, 3): 1, (1, 0): 1, (1, 1): 0, (1, 2): 0, (1, 3): 1}
    order = {0: (1, 3, 2), 1: (0, 1, 3, 2)}

    def y_step1(plane, rs):
        for r in rs:
            ref = keys_ref.at[block(plane, r), core, strip(y)]
            for d in range(2):
                i = (plane * 2 + d) * 4 + r
                go(ref, y1send.at[i], y1got.at[i], to_y[d])

    def y_step2(plane):
        for r in order[plane]:
            for d, source in enumerate((y_down, y_up)):
                i = (plane * 2 + d) * 4 + r
                ref = keys_ref.at[block(plane, r), core, strip(source)]
                got(ref, y1send.at[i], y1got.at[i])
                if onward[(plane, r)] == d:
                    i = plane * 4 + r
                    go(ref, y2send.at[i], y2got.at[i], to_y[d])

    halves = (pl.ds(direct, rows - direct), pl.ds(0, direct))

    def to_sibling(plane, s, r):
        i = (plane * 2 + s) * 4 + r
        ref = keys_ref.at[block(plane, r), core, halves[s]]
        go(ref, csend.at[i], cgot.at[i], to_core)

    def y_finish(plane):
        for r in order[plane]:
            i = plane * 4 + r
            ref = keys_ref.at[block(plane, r), core, strip(y_far)]
            got(ref, y2send.at[i], y2got.at[i])
            to_sibling(plane, 0, r)

    got(keys_ref.at[block(1, 0), core, sets[0]], zsend.at[0], zgot.at[0])
    x_step1(1, 0)
    x_step2(0, 0)
    y_step1(0, (1, 3))
    y_step1(1, (0,))
    got(keys_ref.at[block(1, 0), core, sets[1]], zsend.at[1], zgot.at[1])
    x_step1(1, 1)
    to_sibling(1, 1, 0)
    x_step2(1, 0)
    y_step1(1, (1, 3))
    x_finish(0, 0)
    y_step1(0, (2,))
    x_step2(0, 1)
    to_sibling(0, 1, 1)
    to_sibling(0, 1, 3)
    x_finish(1, 0)
    y_step1(1, (2,))
    y_step2(0)
    x_step2(1, 1)
    to_sibling(1, 1, 1)
    to_sibling(1, 1, 3)
    x_finish(0, 1)
    to_sibling(0, 1, 2)
    y_step2(1)
    y_finish(0)
    x_finish(1, 1)
    to_sibling(1, 1, 2)
    y_finish(1)
    for plane in range(2):
        for s in range(2):
            for r in range(4):
                i = (plane * 2 + s) * 4 + r
                ref = keys_ref.at[block(plane, r), 1 - core, halves[s]]
                got(ref, csend.at[i], cgot.at[i])
    for one in pending:
        one.wait_send()


def gather(by_head, latents, scale_row, w_uk):
    heads, rows, _ = by_head.shape
    width = latents.shape[1]
    dma = pltpu.SemaphoreType.DMA
    vmem = pl.BlockSpec(memory_space=pltpu.VMEM)
    counts = (2, 8, 8, 16, 8, 16)
    return pl.pallas_call(
        gather_kernel,
        out_shape=(
            jax.ShapeDtypeStruct((8, 2, rows, width), jnp.bfloat16),
            jax.ShapeDtypeStruct((heads, rows, width), jnp.bfloat16),
        ),
        in_specs=[vmem] * 4,
        out_specs=(vmem, vmem),
        scratch_shapes=[dma((n,)) for n in counts for _ in range(2)],
        compiler_params=pltpu.CompilerParams(
            collective_id=1, has_side_effects=True, vmem_limit_bytes=20 << 20
        ),
        name="gather",
    )(by_head, latents, scale_row, w_uk)


def shards(query, latents, lat_scale, doc_lengths, w_uk, w_uv, w_o):
    by_head = jnp.transpose(query, (1, 0, 2))
    keys, query_full = gather(by_head, latents, lat_scale.reshape(1, -1), w_uk)
    width = latents.shape[1]
    head_out = attention(
        doc_lengths, query_full.reshape(-1, width), keys.reshape(-1, width), w_uv
    )
    return project_and_reduce(head_out, w_o)


def solution(mesh):
    placed = (
        P("ctx", "head", None),
        P("ctx", None),
        P("ctx"),
        P(),
        P("head", None, None),
        P("head", None, None),
        P("head", None),
    )
    return jax.shard_map(
        shards, mesh=mesh, in_specs=placed, out_specs=P("ctx", "head"), check_vma=False
    )
```

```python
import jax
import jax.numpy as jnp
from jax import lax
from jax.experimental import pallas as pl
from jax.experimental.pallas import tpu as pltpu
from jax.sharding import PartitionSpec as P

LAT = 512
NOPE = 128
QDIM = 192
VDIM = 128
GROUP = 4
NEG = -1e30
MESH = pl.DeviceIdType.MESH
EXP_SCALE = float(QDIM) ** -0.5 * 1.4426950408889634


def attend_kernel(
    lens_hbm, q_hbm, latents_hbm, scale_hbm, uk_hbm, uv_hbm, out_ref,
    lens_ref, q_ref, latents_ref, scale_ref, uk_ref, uv_ref,
    keys_ref, qf_ref, s_ref, m_ref, l_ref, acc_ref, first_ref, load_sem,
    zsend, zgot, x1send, x1got, x2send, x2got, csend, cgot,
):
    rows = latents_ref.shape[1]
    heads = q_ref.shape[0]
    block_rows = GROUP * rows
    groups = heads // GROUP
    ctx = lax.axis_index("ctx")
    head = lax.axis_index("head")
    core = lax.rem(ctx, 2)
    x = lax.rem(ctx // 2, 4)
    hi = ctx // 8
    y = lax.rem(head, 4)
    lo = head // 4
    x_up, x_down, x_far = lax.rem(x + 1, 4), lax.rem(x + 3, 4), lax.rem(x + 2, 4)
    planes = (hi * 4, (1 - hi) * 4)
    around = (x, x_up, x_far, x_down)

    loads = [
        pltpu.make_async_copy(src, dst, load_sem.at[i])
        for i, (src, dst) in enumerate(
            (
                (latents_hbm, latents_ref),
                (scale_hbm, scale_ref),
                (uk_hbm, uk_ref),
                (lens_hbm, lens_ref),
                (uv_hbm, uv_ref),
                (q_hbm, q_ref),
            )
        )
    ]
    for load in loads:
        load.start()

    def place(a, b, c, d, e):
        return {"ctx": a * 8 + b * 2 + c, "head": d * 4 + e}

    to_x = (place(hi, x_up, core, lo, y), place(hi, x_down, core, lo, y))
    to_z = place(1 - hi, x, core, 1 - lo, y)
    to_core = place(hi, x, 1 - core, lo, y)

    def copy(src, dst, ssem, rsem, target):
        return pltpu.make_async_remote_copy(
            src_ref=src, dst_ref=dst, send_sem=ssem, recv_sem=rsem,
            device_id=target, device_id_type=MESH,
        )

    pending = []

    def go(ref, ssem, rsem, target):
        one = copy(ref, ref, ssem, rsem, target)
        one.start()
        pending.append(one)

    def got(ref, ssem, rsem):
        copy(ref, ref, ssem, rsem, to_core).wait_recv()

    barrier = pltpu.get_barrier_semaphore()
    for target in (*to_x, to_z, to_core):
        pl.semaphore_signal(barrier, inc=1, device_id=target, device_id_type=MESH)

    def block(plane, r):
        return planes[plane] + around[r]

    loads[0].wait()
    loads[1].wait()
    mine = block(0, 0)
    latent = latents_ref[...].astype(jnp.float32)
    keys_ref[mine, core, :, :LAT] = (latent[:LAT] * scale_ref[...]).T.astype(jnp.bfloat16)
    keys_ref[mine, core, :, LAT:] = latent[LAT:].T.astype(jnp.bfloat16)

    pl.semaphore_wait(barrier, 4)

    parts = (pl.ds(0, rows // 2), pl.ds(rows // 2, rows // 2))

    def x_step1(plane):
        for d in range(2):
            i = plane * 2 + d
            go(keys_ref.at[block(plane, 0), core], x1send.at[i], x1got.at[i], to_x[d])

    def to_sibling(plane, r):
        i = plane * 4 + r
        go(keys_ref.at[block(plane, r), core], csend.at[i], cgot.at[i], to_core)

    def from_sibling(plane, r):
        i = plane * 4 + r
        got(keys_ref.at[block(plane, r), 1 - core], csend.at[i], cgot.at[i])

    def x_step2(plane):
        for d, r in enumerate((3, 1)):
            i = plane * 2 + d
            got(keys_ref.at[block(plane, r), core], x1send.at[i], x1got.at[i])
            go(keys_ref.at[block(plane, r), core, parts[d]], x2send.at[i], x2got.at[i], to_x[d])
        to_sibling(plane, 1)
        to_sibling(plane, 3)

    def x_finish(plane):
        for d in range(2):
            i = plane * 2 + d
            got(keys_ref.at[block(plane, 2), core, parts[d]], x2send.at[i], x2got.at[i])
        to_sibling(plane, 2)

    def from_z():
        got(keys_ref.at[block(1, 0), core], zsend.at[0], zgot.at[0])
        x_step1(1)
        to_sibling(1, 0)

    go(keys_ref.at[mine, core], zsend.at[0], zgot.at[0], to_z)
    x_step1(0)
    to_sibling(0, 0)

    loads[2].wait()
    loads[5].wait()
    for h in range(heads):
        q = q_ref[h].astype(jnp.float32).T.astype(jnp.bfloat16)
        lat = jnp.dot(q[:, :NOPE], uk_ref[h], preferred_element_type=jnp.float32)
        qf_ref[h, :, :LAT] = lat.astype(jnp.bfloat16)
        qf_ref[h, :, LAT:] = q[:, NOPE:]

    loads[3].wait()
    t0 = ctx * rows
    qpos = t0 + lax.broadcasted_iota(jnp.int32, (rows, 128), 0)
    first = jnp.zeros_like(qpos)
    end = jnp.int32(0)
    for k in range(lens_ref.shape[0]):
        end = end + lens_ref[k]
        first = jnp.where(qpos >= end, end, first)
    first_ref[...] = jnp.concatenate([first] * GROUP, axis=0)
    m_ref[...] = jnp.full_like(m_ref, NEG)

    def scores(p, k, diagonal):
        j = p * 2 + k
        kpos = j * rows + lax.broadcasted_iota(jnp.int32, (1, 128), 1)

        def one_group(g, carry):
            q = qf_ref[pl.ds(g * GROUP, GROUP)].reshape(block_rows, -1)
            s = lax.dot_general(
                q, keys_ref[p, k], (((1,), (1,)), ((), ())), preferred_element_type=jnp.float32
            )
            here = pl.ds(pl.multiple_of(g * block_rows, block_rows), block_rows)
            top = m_ref[here]
            for lane in range(0, rows, 128):
                allowed = first_ref[...] <= kpos + lane
                if diagonal:
                    local = lax.broadcasted_iota(jnp.int32, (block_rows, 128), 0)
                    ahead = lane + lax.broadcasted_iota(jnp.int32, (block_rows, 128), 1)
                    allowed = allowed & (ahead <= lax.rem(local, rows))
                part = jnp.where(allowed, s[:, lane : lane + 128], NEG)
                s_ref[j, here, lane : lane + 128] = part
                top = jnp.maximum(top, part)
            m_ref[here] = top
            return carry

        lax.fori_loop(0, groups, one_group, 0)

    def tiles(plane, r, count, k):
        def one(i, carry):
            p = planes[plane] + lax.rem(x + r + 2 * i, 4)

            @pl.when(p * 2 + k < ctx)
            def _():
                scores(p, k, False)

            return carry

        lax.fori_loop(0, count, one, 0)

    scores(mine, core, True)
    from_z()
    x_step2(0)
    from_sibling(0, 0)
    tiles(0, 0, 1, 1 - core)
    tiles(0, 1, 2, core)
    x_step2(1)
    x_finish(0)
    tiles(1, 0, 1, core)
    for r in (1, 3):
        from_sibling(0, r)
    from_sibling(1, 0)
    tiles(0, 1, 2, 1 - core)
    tiles(1, 0, 1, 1 - core)
    x_finish(1)
    tiles(1, 1, 2, core)
    tiles(0, 2, 1, core)
    for r in (1, 3):
        from_sibling(1, r)
    tiles(1, 1, 2, 1 - core)
    tiles(1, 2, 1, core)
    from_sibling(0, 2)
    from_sibling(1, 2)
    tiles(0, 2, 1, 1 - core)
    tiles(1, 2, 1, 1 - core)

    @pl.when(core == 0)
    def _():
        s_ref[ctx + 1] = jnp.full(s_ref.shape[1:], NEG, jnp.float32)

    loads[4].wait()

    def context_of(g, carry):
        here = pl.ds(pl.multiple_of(g * block_rows, block_rows), block_rows)
        m = jnp.max(m_ref[here], axis=1, keepdims=True)
        m_ref[here] = jnp.broadcast_to(m, (block_rows, 128))
        l_ref[...] = jnp.zeros_like(l_ref)
        acc_ref[...] = jnp.zeros_like(acc_ref)

        def weigh(p, carry):
            top = m_ref[here]
            weights = []
            total = l_ref[...]
            for k in range(2):
                for lane in range(0, rows, 128):
                    s = s_ref[2 * p + k, here, lane : lane + 128]
                    w = jnp.exp2((s - top) * EXP_SCALE)
                    total = total + w
                    weights.append(w.astype(jnp.bfloat16))
            l_ref[...] = total
            values = keys_ref[p, :, :, :LAT].reshape(2 * rows, LAT)
            acc_ref[...] += jnp.dot(
                jnp.concatenate(weights, axis=1), values, preferred_element_type=jnp.float32
            )
            return carry

        lax.fori_loop(0, ctx // 2 + 1, weigh, 0)
        inverse = 1.0 / jnp.sum(l_ref[...], axis=1, keepdims=True)
        context = (acc_ref[...] * inverse).astype(jnp.bfloat16)
        for i in range(GROUP):
            h = g * GROUP + i
            one = jnp.dot(
                context[i * rows : (i + 1) * rows], uv_ref[h], preferred_element_type=jnp.float32
            )
            out_ref[:, pl.ds(pl.multiple_of(h * VDIM, VDIM), VDIM)] = one.astype(jnp.bfloat16)
        return carry

    lax.fori_loop(0, groups, context_of, 0)
    for one in pending:
        one.wait_send()


def attend(doc_lengths, by_head, latents, scale_row, w_uk, w_uv):
    heads, _, rows = by_head.shape
    width = latents.shape[0]
    dma = pltpu.SemaphoreType.DMA
    vmem = pltpu.VMEM
    outside = pl.BlockSpec(memory_space=pl.ANY)
    whole = pl.BlockSpec(memory_space=pltpu.VMEM)
    block_rows = GROUP * rows
    return pl.pallas_call(
        attend_kernel,
        out_shape=jax.ShapeDtypeStruct((rows, heads * VDIM), jnp.bfloat16),
        in_specs=[outside] * 6,
        out_specs=whole,
        scratch_shapes=[
            pltpu.SMEM(doc_lengths.shape, jnp.int32),
            vmem(by_head.shape, by_head.dtype),
            vmem(latents.shape, latents.dtype),
            vmem(scale_row.shape, scale_row.dtype),
            vmem(w_uk.shape, w_uk.dtype),
            vmem(w_uv.shape, w_uv.dtype),
            vmem((8, 2, rows, width), jnp.bfloat16),
            vmem((heads, rows, width), jnp.bfloat16),
            vmem((16, heads * rows, rows), jnp.float32),
            vmem((heads * rows, 128), jnp.float32),
            vmem((block_rows, 128), jnp.float32),
            vmem((block_rows, LAT), jnp.float32),
            vmem((block_rows, 128), jnp.int32),
            dma((6,)),
            dma((1,)), dma((1,)),
            dma((4,)), dma((4,)),
            dma((4,)), dma((4,)),
            dma((8,)), dma((8,)),
        ],
        compiler_params=pltpu.CompilerParams(
            collective_id=1, has_side_effects=True, vmem_limit_bytes=61 << 20
        ),
        name="attend",
    )(doc_lengths, by_head, latents, scale_row, w_uk, w_uv)


def reduce_kernel(
    x_hbm, w_ref, out_ref, x_ref, x_sem, wbuf, own, zrecv, y1recv, y2recv, ysecond1, ysecond2, zlast,
    wsem, zsend, zgot, y1send, y1got, y2send, y2got, s1send, s1got, s2send, s2got, lsend, lgot,
):
    cols = out_ref.shape[1]
    half = out_ref.shape[0] // 2
    quarter = half // 2
    me = lax.axis_index("head")
    y = lax.rem(me, 4)
    z = me // 4
    up = z * 4 + lax.rem(y + 1, 4)
    down = z * 4 + lax.rem(y + 3, 4)
    across = (1 - z) * 4 + y
    blocks = ((2, 0), (2, 1), (1, 0), (3, 0), (1, 1), (3, 1), (0, 0), (0, 1))
    slot = {key: k for k, key in enumerate(blocks)}
    first = pl.ds(0, half)
    second = pl.ds(half, half)

    def fetch(k):
        shift, mine = blocks[k]
        plane = z if mine else 1 - z
        start = pl.multiple_of((plane * 4 + lax.rem(y + shift, 4)) * cols, 128)
        return pltpu.make_async_copy(w_ref.at[:, pl.ds(start, cols)], wbuf.at[k], wsem.at[k])

    def send(src, dst, ssem, rsem, target):
        return pltpu.make_async_remote_copy(
            src_ref=src, dst_ref=dst, send_sem=ssem, recv_sem=rsem,
            device_id={"head": target}, device_id_type=MESH,
        )

    load = pltpu.make_async_copy(x_hbm, x_ref, x_sem.at[0])
    load.start()
    for k in range(8):
        fetch(k).start()
    barrier = pltpu.get_barrier_semaphore()
    for target in (up, down, across):
        pl.semaphore_signal(barrier, inc=1, device_id={"head": target}, device_id_type=MESH)
    load.wait()
    pl.semaphore_wait(barrier, 3)

    pending = []

    def go(copy):
        copy.start()
        pending.append(copy)

    def across_copy(i, k):
        return send(own.at[k, first], zrecv.at[i], zsend.at[i], zgot.at[i], across)

    def step1(k, base, buf, ssem, rsem, i):
        go(send(own.at[k, pl.ds(base, quarter)], buf.at[i], ssem.at[i], rsem.at[i], up))
        go(
            send(
                own.at[k, pl.ds(base + quarter, quarter)],
                buf.at[i + 1], ssem.at[i + 1], rsem.at[i + 1], down,
            )
        )

    across_order = (2, 1, 3, 0)
    across_copies = {}

    def compute(k):
        fetch(k).wait()
        own[k] = jnp.dot(x_ref[...], wbuf[k], preferred_element_type=jnp.float32).astype(
            jnp.bfloat16
        )
        shift, mine = blocks[k]
        if not mine:
            i = across_order.index(shift)
            across_copies[i] = across_copy(i, k)
            go(across_copies[i])
        if shift == 2:
            step1(k, half, y1recv, y1send, y1got, 2 * mine)

    def add_rows(k, rows, *terms):
        total = own[k, rows].astype(jnp.float32)
        for term in terms:
            total = total + term.astype(jnp.float32)
        return total

    copies = {}

    def y_first_step2(mine):
        for side, (shift, target, offset) in enumerate(((1, up, 0), (3, down, quarter))):
            k = slot[(shift, mine)]
            i = 2 * mine + side
            rows = pl.ds(half + offset, quarter)
            send(
                own.at[0, pl.ds(0, quarter)], y1recv.at[i], y1send.at[i], y1got.at[i], target
            ).wait_recv()
            own[k, rows] = add_rows(k, rows, y1recv[i]).astype(jnp.bfloat16)
            go(send(own.at[k, second], y2recv.at[i], y2send.at[i], y2got.at[i], target))

    def got(buf, i, ssem, rsem, rows):
        send(own.at[0, pl.ds(0, rows)], buf.at[i], ssem.at[i], rsem.at[i], across).wait_recv()

    for k in range(6):
        compute(k)
    y_first_step2(0)
    for k in range(6, 8):
        compute(k)
    y_first_step2(1)

    got(zrecv, 0, zsend, zgot, half)
    k = slot[(2, 1)]
    own[k, first] = add_rows(k, first, zrecv[0]).astype(jnp.bfloat16)
    step1(k, 0, ysecond1, s1send, s1got, 0)

    got(y2recv, 0, y2send, y2got, half)
    got(y2recv, 1, y2send, y2got, half)
    k = slot[(0, 0)]
    own[k, second] = add_rows(k, second, y2recv[0], y2recv[1]).astype(jnp.bfloat16)
    go(send(own.at[k, second], zlast.at[0], lsend.at[0], lgot.at[0], across))

    for side, (shift, target, offset) in enumerate(((1, up, 0), (3, down, quarter))):
        k = slot[(shift, 1)]
        got(zrecv, 1 + side, zsend, zgot, half)
        got(ysecond1, side, s1send, s1got, quarter)
        own[k, first] = add_rows(k, first, zrecv[1 + side]).astype(jnp.bfloat16)
        rows = pl.ds(offset, quarter)
        own[k, rows] = add_rows(k, rows, ysecond1[side]).astype(jnp.bfloat16)
        go(send(own.at[k, first], ysecond2.at[side], s2send.at[side], s2got.at[side], target))

    k = slot[(0, 1)]
    got(y2recv, 2, y2send, y2got, half)
    got(y2recv, 3, y2send, y2got, half)
    got(zlast, 0, lsend, lgot, half)
    out_ref[second] = add_rows(k, second, y2recv[2], y2recv[3], zlast[0]).astype(jnp.bfloat16)
    got(zrecv, 3, zsend, zgot, half)
    got(ysecond2, 0, s2send, s2got, half)
    got(ysecond2, 1, s2send, s2got, half)
    out_ref[first] = add_rows(k, first, zrecv[3], ysecond2[0], ysecond2[1]).astype(jnp.bfloat16)
    for copy in pending:
        copy.wait_send()


def project_and_reduce(head_out, w_o):
    rows, inner = head_out.shape
    cols = w_o.shape[1] // 8
    half = rows // 2
    dma = pltpu.SemaphoreType.DMA
    return pl.pallas_call(
        reduce_kernel,
        out_shape=jax.ShapeDtypeStruct((rows, cols), jnp.bfloat16),
        in_specs=[pl.BlockSpec(memory_space=pl.ANY)] * 2,
        out_specs=pl.BlockSpec(memory_space=pltpu.VMEM),
        scratch_shapes=[
            pltpu.VMEM((rows, inner), jnp.bfloat16),
            dma((1,)),
            pltpu.VMEM((8, inner, cols), jnp.bfloat16),
            pltpu.VMEM((8, rows, cols), jnp.bfloat16),
            pltpu.VMEM((4, half, cols), jnp.bfloat16),
            pltpu.VMEM((4, half // 2, cols), jnp.bfloat16),
            pltpu.VMEM((4, half, cols), jnp.bfloat16),
            pltpu.VMEM((2, half // 2, cols), jnp.bfloat16),
            pltpu.VMEM((2, half, cols), jnp.bfloat16),
            pltpu.VMEM((1, half, cols), jnp.bfloat16),
            dma((8,)),
            dma((4,)), dma((4,)),
            dma((4,)), dma((4,)),
            dma((4,)), dma((4,)),
            dma((2,)), dma((2,)),
            dma((2,)), dma((2,)),
            dma((1,)), dma((1,)),
        ],
        compiler_params=pltpu.CompilerParams(
            collective_id=0, has_side_effects=True, vmem_limit_bytes=40 << 20
        ),
        name="project_and_reduce",
    )(head_out, w_o)


def shards(query, latents, lat_scale, doc_lengths, w_uk, w_uv, w_o):
    by_head = jnp.transpose(query, (1, 2, 0))
    head_out = attend(doc_lengths, by_head, latents.T, lat_scale.reshape(1, -1), w_uk, w_uv)
    return project_and_reduce(head_out, w_o)


def solution(mesh):
    placed = (
        P("ctx", "head", None),
        P("ctx", None),
        P("ctx"),
        P(),
        P("head", None, None),
        P("head", None, None),
        P("head", None),
    )
    return jax.shard_map(
        shards, mesh=mesh, in_specs=placed, out_specs=P("ctx", "head"), check_vma=False
    )
```

```python
import jax
import jax.numpy as jnp
from jax import lax
from jax.experimental import pallas as pl
from jax.experimental.pallas import tpu as pltpu
from jax.sharding import PartitionSpec as P

LAT = 512
NOPE = 128
QDIM = 192
VDIM = 128
GROUP = 4
NEG = -1e30
MESH = pl.DeviceIdType.MESH
EXP_SCALE = float(QDIM) ** -0.5 * 1.4426950408889634


def attend_kernel(
    lens_hbm, q_hbm, latents_hbm, scale_hbm, uk_hbm, uv_hbm, out_ref,
    lens_ref, q_ref, latents_ref, scale_ref, uk_ref, uv_ref,
    keys_ref, qf_ref, s_ref, m_ref, l_ref, acc_ref, first_ref, load_sem,
    zsend, zgot, x1send, x1got, x2send, x2got, s1send, s1got, s2send, s2got,
    y1send, y1got, y2send, y2got, csend, cgot,
):
    rows = latents_ref.shape[1]
    heads = q_ref.shape[0]
    block_rows = GROUP * rows
    groups = heads // GROUP
    ctx = lax.axis_index("ctx")
    head = lax.axis_index("head")
    core = lax.rem(ctx, 2)
    x = lax.rem(ctx // 2, 4)
    hi = ctx // 8
    y = lax.rem(head, 4)
    lo = head // 4
    x_up, x_down, x_far = lax.rem(x + 1, 4), lax.rem(x + 3, 4), lax.rem(x + 2, 4)
    y_up, y_down, y_far = lax.rem(y + 1, 4), lax.rem(y + 3, 4), lax.rem(y + 2, 4)
    planes = (hi * 4, (1 - hi) * 4)
    around = (x, x_up, x_far, x_down)

    loads = [
        pltpu.make_async_copy(src, dst, load_sem.at[i])
        for i, (src, dst) in enumerate(
            (
                (latents_hbm, latents_ref),
                (scale_hbm, scale_ref),
                (uk_hbm, uk_ref),
                (lens_hbm, lens_ref),
                (uv_hbm, uv_ref),
                (q_hbm, q_ref),
            )
        )
    ]
    for load in loads:
        load.start()

    def place(a, b, c, d, e):
        return {"ctx": a * 8 + b * 2 + c, "head": d * 4 + e}

    to_x = (place(hi, x_up, core, lo, y), place(hi, x_down, core, lo, y))
    to_y = (place(hi, x, core, lo, y_up), place(hi, x, core, lo, y_down))
    to_z = place(1 - hi, x, core, 1 - lo, y)
    to_core = place(hi, x, 1 - core, lo, y)

    def copy(src, dst, ssem, rsem, target):
        return pltpu.make_async_remote_copy(
            src_ref=src, dst_ref=dst, send_sem=ssem, recv_sem=rsem,
            device_id=target, device_id_type=MESH,
        )

    pending = []

    def go(ref, ssem, rsem, target):
        one = copy(ref, ref, ssem, rsem, target)
        one.start()
        pending.append(one)

    def got(ref, ssem, rsem):
        copy(ref, ref, ssem, rsem, to_core).wait_recv()

    barrier = pltpu.get_barrier_semaphore()
    for target in (*to_x, *to_y, to_z, to_core):
        pl.semaphore_signal(barrier, inc=1, device_id=target, device_id_type=MESH)

    def block(plane, r):
        return planes[plane] + around[r]

    loads[0].wait()
    loads[1].wait()
    mine = block(0, 0)
    latent = latents_ref[...].astype(jnp.float32)
    keys_ref[mine, core, :, :LAT] = (latent[:LAT] * scale_ref[...]).T.astype(jnp.bfloat16)
    keys_ref[mine, core, :, LAT:] = latent[LAT:].T.astype(jnp.bfloat16)

    pl.semaphore_wait(barrier, 6)

    parts = (pl.ds(0, rows // 2), pl.ds(rows // 2, rows // 2))
    width = rows // 4

    def strip(index):
        return pl.ds(pl.multiple_of(index * width, 16), width)

    def strip_half(index, which):
        return pl.ds(pl.multiple_of(index * width + which * (width // 2), 16), width // 2)

    def at(plane, r, part):
        return keys_ref.at[block(plane, r), core, part]

    def to_sibling(plane, r):
        i = plane * 4 + r
        go(keys_ref.at[block(plane, r), core], csend.at[i], cgot.at[i], to_core)

    def from_sibling(plane, r):
        i = plane * 4 + r
        got(keys_ref.at[block(plane, r), 1 - core], csend.at[i], cgot.at[i])

    origin = (3, 1)

    def own_first():
        for d in range(2):
            go(at(0, 0, parts[d]), x1send.at[d], x1got.at[d], to_x[d])

    def own_second():
        for d in range(2):
            go(at(0, 0, parts[1 - d]), x1send.at[2 + d], x1got.at[2 + d], to_x[d])

    def own_onward():
        for d in range(2):
            ref = at(0, origin[d], parts[d])
            got(ref, x1send.at[d], x1got.at[d])
            go(ref, x2send.at[d], x2got.at[d], to_x[d])

    def own_near():
        for d in range(2):
            got(at(0, origin[d], parts[1 - d]), x1send.at[2 + d], x1got.at[2 + d])
            to_sibling(0, origin[d])

    def own_far():
        for d in range(2):
            got(at(0, 2, parts[d]), x2send.at[d], x2got.at[d])
        to_sibling(0, 2)

    def y_step1(r):
        for d in range(2):
            i = r * 2 + d
            go(at(1, r, strip(y)), y1send.at[i], y1got.at[i], to_y[d])

    def from_z():
        got(at(1, 0, strip(y)), zsend.at[0], zgot.at[0])
        for d in range(2):
            go(at(1, 0, strip(y)), s1send.at[d], s1got.at[d], to_x[d])
        y_step1(0)

    def strips_onward():
        for d in range(2):
            got(at(1, origin[d], strip(y)), s1send.at[d], s1got.at[d])
            go(at(1, origin[d], strip_half(y, d)), s2send.at[d], s2got.at[d], to_x[d])
        y_step1(1)
        y_step1(3)

    def strips_far():
        for d in range(2):
            got(at(1, 2, strip_half(y, d)), s2send.at[d], s2got.at[d])
        y_step1(2)

    def y_step2(r):
        for d, source in enumerate((y_down, y_up)):
            i = r * 2 + d
            got(at(1, r, strip(source)), y1send.at[i], y1got.at[i])
            go(at(1, r, strip_half(source, d)), y2send.at[i], y2got.at[i], to_y[d])

    def y_finish(r):
        for d in range(2):
            i = r * 2 + d
            got(at(1, r, strip_half(y_far, d)), y2send.at[i], y2got.at[i])
        to_sibling(1, r)

    def queries(start, stop):
        for h in range(start, stop):
            q = q_ref[h].astype(jnp.float32).T.astype(jnp.bfloat16)
            lat = jnp.dot(q[:, :NOPE], uk_ref[h], preferred_element_type=jnp.float32)
            qf_ref[h, :, :LAT] = lat.astype(jnp.bfloat16)
            qf_ref[h, :, LAT:] = q[:, NOPE:]

    go(at(0, 0, strip(y)), zsend.at[0], zgot.at[0], to_z)
    own_first()
    to_sibling(0, 0)
    loads[2].wait()
    loads[5].wait()
    queries(0, heads // 2)
    from_z()
    own_second()
    queries(heads // 2, heads)

    loads[3].wait()
    t0 = ctx * rows
    qpos = t0 + lax.broadcasted_iota(jnp.int32, (rows, 128), 0)
    first = jnp.zeros_like(qpos)
    end = jnp.int32(0)
    for k in range(lens_ref.shape[0]):
        end = end + lens_ref[k]
        first = jnp.where(qpos >= end, end, first)
    first_ref[...] = jnp.concatenate([first] * GROUP, axis=0)
    m_ref[...] = jnp.full_like(m_ref, NEG)

    def scores(p, k, diagonal):
        j = p * 2 + k
        kpos = j * rows + lax.broadcasted_iota(jnp.int32, (1, 128), 1)

        def one_group(g, carry):
            q = qf_ref[pl.ds(g * GROUP, GROUP)].reshape(block_rows, -1)
            s = lax.dot_general(
                q, keys_ref[p, k], (((1,), (1,)), ((), ())), preferred_element_type=jnp.float32
            )
            here = pl.ds(pl.multiple_of(g * block_rows, block_rows), block_rows)
            top = m_ref[here]
            for lane in range(0, rows, 128):
                allowed = first_ref[...] <= kpos + lane
                if diagonal:
                    local = lax.broadcasted_iota(jnp.int32, (block_rows, 128), 0)
                    ahead = lane + lax.broadcasted_iota(jnp.int32, (block_rows, 128), 1)
                    allowed = allowed & (ahead <= lax.rem(local, rows))
                part = jnp.where(allowed, s[:, lane : lane + 128], NEG)
                s_ref[j, here, lane : lane + 128] = part
                top = jnp.maximum(top, part)
            m_ref[here] = top
            return carry

        lax.fori_loop(0, groups, one_group, 0)

    def tiles(plane, r, count, k):
        def one(i, carry):
            p = planes[plane] + lax.rem(x + r + 2 * i, 4)

            @pl.when(p * 2 + k < ctx)
            def _():
                scores(p, k, False)

            return carry

        lax.fori_loop(0, count, one, 0)

    scores(mine, core, True)
    strips_onward()
    own_onward()
    from_sibling(0, 0)
    tiles(0, 0, 1, 1 - core)
    y_step2(0)
    strips_far()
    own_near()
    y_step2(1)
    y_step2(3)
    tiles(0, 1, 2, core)
    y_finish(0)
    own_far()
    y_step2(2)
    tiles(1, 0, 1, core)
    from_sibling(0, 1)
    from_sibling(0, 3)
    y_finish(1)
    y_finish(3)
    tiles(0, 1, 2, 1 - core)
    tiles(0, 2, 1, core)
    y_finish(2)
    from_sibling(1, 0)
    tiles(1, 0, 1, 1 - core)
    tiles(1, 1, 2, core)
    from_sibling(0, 2)
    tiles(0, 2, 1, 1 - core)
    from_sibling(1, 1)
    from_sibling(1, 3)
    tiles(1, 1, 2, 1 - core)
    tiles(1, 2, 1, core)
    from_sibling(1, 2)
    tiles(1, 2, 1, 1 - core)

    @pl.when(core == 0)
    def _():
        s_ref[ctx + 1] = jnp.full(s_ref.shape[1:], NEG, jnp.float32)

    loads[4].wait()

    def context_of(g, carry):
        here = pl.ds(pl.multiple_of(g * block_rows, block_rows), block_rows)
        m = jnp.max(m_ref[here], axis=1, keepdims=True)
        m_ref[here] = jnp.broadcast_to(m, (block_rows, 128))
        l_ref[...] = jnp.zeros_like(l_ref)
        acc_ref[...] = jnp.zeros_like(acc_ref)

        def weigh(p, carry):
            top = m_ref[here]
            weights = []
            total = l_ref[...]
            for k in range(2):
                for lane in range(0, rows, 128):
                    s = s_ref[2 * p + k, here, lane : lane + 128]
                    w = jnp.exp2((s - top) * EXP_SCALE)
                    total = total + w
                    weights.append(w.astype(jnp.bfloat16))
            l_ref[...] = total
            values = keys_ref[p, :, :, :LAT].reshape(2 * rows, LAT)
            acc_ref[...] += jnp.dot(
                jnp.concatenate(weights, axis=1), values, preferred_element_type=jnp.float32
            )
            return carry

        lax.fori_loop(0, ctx // 2 + 1, weigh, 0)
        inverse = 1.0 / jnp.sum(l_ref[...], axis=1, keepdims=True)
        context = (acc_ref[...] * inverse).astype(jnp.bfloat16)
        for i in range(GROUP):
            h = g * GROUP + i
            one = jnp.dot(
                context[i * rows : (i + 1) * rows], uv_ref[h], preferred_element_type=jnp.float32
            )
            out_ref[:, pl.ds(pl.multiple_of(h * VDIM, VDIM), VDIM)] = one.astype(jnp.bfloat16)
        return carry

    lax.fori_loop(0, groups, context_of, 0)
    for one in pending:
        one.wait_send()


def attend(doc_lengths, by_head, latents, scale_row, w_uk, w_uv):
    heads, _, rows = by_head.shape
    width = latents.shape[0]
    dma = pltpu.SemaphoreType.DMA
    vmem = pltpu.VMEM
    outside = pl.BlockSpec(memory_space=pl.ANY)
    whole = pl.BlockSpec(memory_space=pltpu.VMEM)
    block_rows = GROUP * rows
    return pl.pallas_call(
        attend_kernel,
        out_shape=jax.ShapeDtypeStruct((rows, heads * VDIM), jnp.bfloat16),
        in_specs=[outside] * 6,
        out_specs=whole,
        scratch_shapes=[
            pltpu.SMEM(doc_lengths.shape, jnp.int32),
            vmem(by_head.shape, by_head.dtype),
            vmem(latents.shape, latents.dtype),
            vmem(scale_row.shape, scale_row.dtype),
            vmem(w_uk.shape, w_uk.dtype),
            vmem(w_uv.shape, w_uv.dtype),
            vmem((8, 2, rows, width), jnp.bfloat16),
            vmem((heads, rows, width), jnp.bfloat16),
            vmem((16, heads * rows, rows), jnp.float32),
            vmem((heads * rows, 128), jnp.float32),
            vmem((block_rows, 128), jnp.float32),
            vmem((block_rows, LAT), jnp.float32),
            vmem((block_rows, 128), jnp.int32),
            dma((6,)),
            dma((1,)), dma((1,)),
            dma((4,)), dma((4,)),
            dma((2,)), dma((2,)),
            dma((2,)), dma((2,)),
            dma((2,)), dma((2,)),
            dma((8,)), dma((8,)),
            dma((8,)), dma((8,)),
            dma((8,)), dma((8,)),
        ],
        compiler_params=pltpu.CompilerParams(
            collective_id=1, has_side_effects=True, vmem_limit_bytes=61 << 20
        ),
        name="attend",
    )(doc_lengths, by_head, latents, scale_row, w_uk, w_uv)


def reduce_kernel(
    x_hbm, w_ref, out_ref, x_ref, x_sem, wbuf, own, zrecv, y1recv, y2recv, ysecond1, ysecond2, zlast,
    wsem, zsend, zgot, y1send, y1got, y2send, y2got, s1send, s1got, s2send, s2got, lsend, lgot,
):
    cols = out_ref.shape[1]
    half = out_ref.shape[0] // 2
    quarter = half // 2
    me = lax.axis_index("head")
    y = lax.rem(me, 4)
    z = me // 4
    up = z * 4 + lax.rem(y + 1, 4)
    down = z * 4 + lax.rem(y + 3, 4)
    across = (1 - z) * 4 + y
    blocks = ((2, 0), (2, 1), (1, 0), (3, 0), (1, 1), (3, 1), (0, 0), (0, 1))
    slot = {key: k for k, key in enumerate(blocks)}
    first = pl.ds(0, half)
    second = pl.ds(half, half)

    def fetch(k):
        shift, mine = blocks[k]
        plane = z if mine else 1 - z
        start = pl.multiple_of((plane * 4 + lax.rem(y + shift, 4)) * cols, 128)
        return pltpu.make_async_copy(w_ref.at[:, pl.ds(start, cols)], wbuf.at[k], wsem.at[k])

    def send(src, dst, ssem, rsem, target):
        return pltpu.make_async_remote_copy(
            src_ref=src, dst_ref=dst, send_sem=ssem, recv_sem=rsem,
            device_id={"head": target}, device_id_type=MESH,
        )

    load = pltpu.make_async_copy(x_hbm, x_ref, x_sem.at[0])
    load.start()
    for k in range(8):
        fetch(k).start()
    barrier = pltpu.get_barrier_semaphore()
    for target in (up, down, across):
        pl.semaphore_signal(barrier, inc=1, device_id={"head": target}, device_id_type=MESH)
    load.wait()
    pl.semaphore_wait(barrier, 3)

    pending = []

    def go(copy):
        copy.start()
        pending.append(copy)

    def across_copy(i, k):
        return send(own.at[k, first], zrecv.at[i], zsend.at[i], zgot.at[i], across)

    def step1(k, base, buf, ssem, rsem, i):
        go(send(own.at[k, pl.ds(base, quarter)], buf.at[i], ssem.at[i], rsem.at[i], up))
        go(
            send(
                own.at[k, pl.ds(base + quarter, quarter)],
                buf.at[i + 1], ssem.at[i + 1], rsem.at[i + 1], down,
            )
        )

    across_order = (2, 1, 3, 0)
    across_copies = {}

    def compute(k):
        fetch(k).wait()
        own[k] = jnp.dot(x_ref[...], wbuf[k], preferred_element_type=jnp.float32).astype(
            jnp.bfloat16
        )
        shift, mine = blocks[k]
        if not mine:
            i = across_order.index(shift)
            across_copies[i] = across_copy(i, k)
            go(across_copies[i])
        if shift == 2:
            step1(k, half, y1recv, y1send, y1got, 2 * mine)

    def add_rows(k, rows, *terms):
        total = own[k, rows].astype(jnp.float32)
        for term in terms:
            total = total + term.astype(jnp.float32)
        return total

    copies = {}

    def y_first_step2(mine):
        for side, (shift, target, offset) in enumerate(((1, up, 0), (3, down, quarter))):
            k = slot[(shift, mine)]
            i = 2 * mine + side
            rows = pl.ds(half + offset, quarter)
            send(
                own.at[0, pl.ds(0, quarter)], y1recv.at[i], y1send.at[i], y1got.at[i], target
            ).wait_recv()
            own[k, rows] = add_rows(k, rows, y1recv[i]).astype(jnp.bfloat16)
            go(send(own.at[k, second], y2recv.at[i], y2send.at[i], y2got.at[i], target))

    def got(buf, i, ssem, rsem, rows):
        send(own.at[0, pl.ds(0, rows)], buf.at[i], ssem.at[i], rsem.at[i], across).wait_recv()

    for k in range(6):
        compute(k)
    y_first_step2(0)
    for k in range(6, 8):
        compute(k)
    y_first_step2(1)

    got(zrecv, 0, zsend, zgot, half)
    k = slot[(2, 1)]
    own[k, first] = add_rows(k, first, zrecv[0]).astype(jnp.bfloat16)
    step1(k, 0, ysecond1, s1send, s1got, 0)

    got(y2recv, 0, y2send, y2got, half)
    got(y2recv, 1, y2send, y2got, half)
    k = slot[(0, 0)]
    own[k, second] = add_rows(k, second, y2recv[0], y2recv[1]).astype(jnp.bfloat16)
    go(send(own.at[k, second], zlast.at[0], lsend.at[0], lgot.at[0], across))

    for side, (shift, target, offset) in enumerate(((1, up, 0), (3, down, quarter))):
        k = slot[(shift, 1)]
        got(zrecv, 1 + side, zsend, zgot, half)
        got(ysecond1, side, s1send, s1got, quarter)
        own[k, first] = add_rows(k, first, zrecv[1 + side]).astype(jnp.bfloat16)
        rows = pl.ds(offset, quarter)
        own[k, rows] = add_rows(k, rows, ysecond1[side]).astype(jnp.bfloat16)
        go(send(own.at[k, first], ysecond2.at[side], s2send.at[side], s2got.at[side], target))

    k = slot[(0, 1)]
    got(y2recv, 2, y2send, y2got, half)
    got(y2recv, 3, y2send, y2got, half)
    got(zlast, 0, lsend, lgot, half)
    out_ref[second] = add_rows(k, second, y2recv[2], y2recv[3], zlast[0]).astype(jnp.bfloat16)
    got(zrecv, 3, zsend, zgot, half)
    got(ysecond2, 0, s2send, s2got, half)
    got(ysecond2, 1, s2send, s2got, half)
    out_ref[first] = add_rows(k, first, zrecv[3], ysecond2[0], ysecond2[1]).astype(jnp.bfloat16)
    for copy in pending:
        copy.wait_send()


def project_and_reduce(head_out, w_o):
    rows, inner = head_out.shape
    cols = w_o.shape[1] // 8
    half = rows // 2
    dma = pltpu.SemaphoreType.DMA
    return pl.pallas_call(
        reduce_kernel,
        out_shape=jax.ShapeDtypeStruct((rows, cols), jnp.bfloat16),
        in_specs=[pl.BlockSpec(memory_space=pltpu.HBM)] * 2,
        out_specs=pl.BlockSpec(memory_space=pltpu.VMEM),
        scratch_shapes=[
            pltpu.VMEM((rows, inner), jnp.bfloat16),
            dma((1,)),
            pltpu.VMEM((8, inner, cols), jnp.bfloat16),
            pltpu.VMEM((8, rows, cols), jnp.bfloat16),
            pltpu.VMEM((4, half, cols), jnp.bfloat16),
            pltpu.VMEM((4, half // 2, cols), jnp.bfloat16),
            pltpu.VMEM((4, half, cols), jnp.bfloat16),
            pltpu.VMEM((2, half // 2, cols), jnp.bfloat16),
            pltpu.VMEM((2, half, cols), jnp.bfloat16),
            pltpu.VMEM((1, half, cols), jnp.bfloat16),
            dma((8,)),
            dma((4,)), dma((4,)),
            dma((4,)), dma((4,)),
            dma((4,)), dma((4,)),
            dma((2,)), dma((2,)),
            dma((2,)), dma((2,)),
            dma((1,)), dma((1,)),
        ],
        compiler_params=pltpu.CompilerParams(
            collective_id=0, has_side_effects=True, vmem_limit_bytes=40 << 20
        ),
        name="project_and_reduce",
    )(head_out, w_o)


def shards(query, latents, lat_scale, doc_lengths, w_uk, w_uv, w_o):
    by_head = jnp.transpose(query, (1, 2, 0))
    head_out = attend(doc_lengths, by_head, latents.T, lat_scale.reshape(1, -1), w_uk, w_uv)
    return project_and_reduce(head_out, w_o)


def solution(mesh):
    placed = (
        P("ctx", "head", None),
        P("ctx", None),
        P("ctx"),
        P(),
        P("head", None, None),
        P("head", None, None),
        P("head", None),
    )
    return jax.shard_map(
        shards, mesh=mesh, in_specs=placed, out_specs=P("ctx", "head"), check_vma=False
    )
```

```python
import jax
import jax.numpy as jnp
from jax import lax
from jax.experimental import pallas as pl
from jax.experimental.pallas import tpu as pltpu
from jax.sharding import PartitionSpec as P

LAT = 512
NOPE = 128
QDIM = 192
VDIM = 128
GROUP = 4
NEG = -1e30
TOO_FAR = 1 << 20
MESH = pl.DeviceIdType.MESH
EXP_SCALE = float(QDIM) ** -0.5 * 1.4426950408889634


def attend_kernel(
    lens_hbm, q_hbm, latents_hbm, scale_hbm, uk_hbm, uv_hbm, out_ref,
    lens_ref, q_ref, latents_ref, scale_ref, uk_ref, uv_ref,
    keys_ref, qf_ref, s_ref, m_ref, l_ref, acc_ref, first_ref, load_sem,
    zsend, zgot, x1send, x1got, x2send, x2got, s1send, s1got, s2send, s2got,
    y1send, y1got, y2send, y2got, csend, cgot, hsend, hgot,
):
    rows = latents_ref.shape[1]
    heads = q_ref.shape[0]
    block_rows = GROUP * rows
    groups = heads // GROUP
    ctx = lax.axis_index("ctx")
    head = lax.axis_index("head")
    core = lax.rem(ctx, 2)
    x = lax.rem(ctx // 2, 4)
    hi = ctx // 8
    y = lax.rem(head, 4)
    lo = head // 4
    x_up, x_down, x_far = lax.rem(x + 1, 4), lax.rem(x + 3, 4), lax.rem(x + 2, 4)
    y_up, y_down, y_far = lax.rem(y + 1, 4), lax.rem(y + 3, 4), lax.rem(y + 2, 4)
    planes = (hi * 4, (1 - hi) * 4)
    around = (x, x_up, x_far, x_down)

    loads = [
        pltpu.make_async_copy(src, dst, load_sem.at[i])
        for i, (src, dst) in enumerate(
            (
                (latents_hbm, latents_ref),
                (scale_hbm, scale_ref),
                (uk_hbm, uk_ref),
                (lens_hbm, lens_ref),
                (uv_hbm, uv_ref),
                (q_hbm, q_ref),
            )
        )
    ]
    for load in loads:
        load.start()

    def place(a, b, c, d, e):
        return {"ctx": a * 8 + b * 2 + c, "head": d * 4 + e}

    to_x = (place(hi, x_up, core, lo, y), place(hi, x_down, core, lo, y))
    to_y = (place(hi, x, core, lo, y_up), place(hi, x, core, lo, y_down))
    to_z = place(1 - hi, x, core, 1 - lo, y)
    to_core = place(hi, x, 1 - core, lo, y)

    def copy(src, dst, ssem, rsem, target):
        return pltpu.make_async_remote_copy(
            src_ref=src, dst_ref=dst, send_sem=ssem, recv_sem=rsem,
            device_id=target, device_id_type=MESH,
        )

    pending = []

    def go(ref, ssem, rsem, target):
        one = copy(ref, ref, ssem, rsem, target)
        one.start()
        pending.append(one)

    def got(ref, ssem, rsem):
        copy(ref, ref, ssem, rsem, to_core).wait_recv()

    barrier = pltpu.get_barrier_semaphore()
    for target in (*to_x, *to_y, to_z, to_core):
        pl.semaphore_signal(barrier, inc=1, device_id=target, device_id_type=MESH)

    def block(plane, r):
        return planes[plane] + around[r]

    loads[0].wait()
    loads[1].wait()
    mine = block(0, 0)
    latent = latents_ref[...].astype(jnp.float32)
    keys_ref[mine, core, :, :LAT] = (latent[:LAT] * scale_ref[...]).T.astype(jnp.bfloat16)
    keys_ref[mine, core, :, LAT:] = latent[LAT:].T.astype(jnp.bfloat16)

    pl.semaphore_wait(barrier, 6)

    parts = (pl.ds(0, rows // 2), pl.ds(rows // 2, rows // 2))
    width = rows // 4

    def strip(index):
        return pl.ds(pl.multiple_of(index * width, 16), width)

    def strip_half(index, which):
        return pl.ds(pl.multiple_of(index * width + which * (width // 2), 16), width // 2)

    def at(plane, r, part):
        return keys_ref.at[block(plane, r), core, part]

    def to_sibling(plane, r):
        i = plane * 4 + r
        go(keys_ref.at[block(plane, r), core], csend.at[i], cgot.at[i], to_core)

    def from_sibling(plane, r):
        i = plane * 4 + r
        got(keys_ref.at[block(plane, r), 1 - core], csend.at[i], cgot.at[i])

    origin = (3, 1)

    def own_first():
        for d in range(2):
            go(at(0, 0, parts[d]), x1send.at[d], x1got.at[d], to_x[d])

    def own_second():
        for d in range(2):
            go(at(0, 0, parts[1 - d]), x1send.at[2 + d], x1got.at[2 + d], to_x[d])

    def near(turn, d):
        return at(0, origin[d], parts[d if turn == 0 else 1 - d])

    def half_to_sibling(turn):
        for d in range(2):
            i = turn * 2 + d
            go(near(turn, d), hsend.at[i], hgot.at[i], to_core)

    def half_from_sibling(turn):
        for d in range(2):
            i = turn * 2 + d
            ref = keys_ref.at[block(0, origin[d]), 1 - core, parts[d if turn == 0 else 1 - d]]
            got(ref, hsend.at[i], hgot.at[i])

    def own_onward():
        for d in range(2):
            got(near(0, d), x1send.at[d], x1got.at[d])
            go(near(0, d), x2send.at[d], x2got.at[d], to_x[d])
        half_to_sibling(0)

    def own_near():
        for d in range(2):
            got(near(1, d), x1send.at[2 + d], x1got.at[2 + d])
        half_to_sibling(1)

    def own_far():
        for d in range(2):
            got(at(0, 2, parts[d]), x2send.at[d], x2got.at[d])
        to_sibling(0, 2)

    def y_step1(r):
        for d in range(2):
            i = r * 2 + d
            go(at(1, r, strip(y)), y1send.at[i], y1got.at[i], to_y[d])

    def from_z():
        got(at(1, 0, strip(y)), zsend.at[0], zgot.at[0])
        for d in range(2):
            go(at(1, 0, strip(y)), s1send.at[d], s1got.at[d], to_x[d])
        y_step1(0)

    def strips_onward():
        for d in range(2):
            got(at(1, origin[d], strip(y)), s1send.at[d], s1got.at[d])
            go(at(1, origin[d], strip_half(y, d)), s2send.at[d], s2got.at[d], to_x[d])
        y_step1(1)
        y_step1(3)

    def strips_far():
        for d in range(2):
            got(at(1, 2, strip_half(y, d)), s2send.at[d], s2got.at[d])
        y_step1(2)

    def y_step2(r):
        for d, source in enumerate((y_down, y_up)):
            i = r * 2 + d
            got(at(1, r, strip(source)), y1send.at[i], y1got.at[i])
            go(at(1, r, strip_half(source, d)), y2send.at[i], y2got.at[i], to_y[d])

    def y_finish(r):
        for d in range(2):
            i = r * 2 + d
            got(at(1, r, strip_half(y_far, d)), y2send.at[i], y2got.at[i])
        to_sibling(1, r)

    def queries():
        for h in range(heads):
            q = q_ref[h].astype(jnp.float32).T.astype(jnp.bfloat16)
            lat = jnp.dot(q[:, :NOPE], uk_ref[h], preferred_element_type=jnp.float32)
            qf_ref[h, :, :LAT] = lat.astype(jnp.bfloat16)
            qf_ref[h, :, LAT:] = q[:, NOPE:]

    go(at(0, 0, strip(y)), zsend.at[0], zgot.at[0], to_z)
    own_first()
    to_sibling(0, 0)
    loads[2].wait()
    loads[5].wait()
    queries()
    from_z()
    own_second()

    loads[3].wait()
    t0 = ctx * rows
    qpos = t0 + lax.broadcasted_iota(jnp.int32, (rows, 128), 0)
    first = jnp.zeros_like(qpos)
    end = jnp.int32(0)
    for k in range(lens_ref.shape[0]):
        end = end + lens_ref[k]
        first = jnp.where(qpos >= end, end, first)
    first_ref[...] = jnp.concatenate([first] * GROUP, axis=0)
    m_ref[...] = jnp.full_like(m_ref, NEG)

    lane_iota = lax.broadcasted_iota(jnp.int32, (1, 128), 1)

    def scores(pieces, whole, diagonal=False):
        def one_group(g, carry):
            q = qf_ref[pl.ds(g * GROUP, GROUP)].reshape(block_rows, -1)
            if whole:
                keys = keys_ref[pieces[0][0], pieces[0][1]]
            else:
                keys = jnp.concatenate([keys_ref[p, k, parts[part]] for p, k, part in pieces], axis=0)
            s = lax.dot_general(
                q, keys, (((1,), (1,)), ((), ())), preferred_element_type=jnp.float32
            )
            here = pl.ds(pl.multiple_of(g * block_rows, block_rows), block_rows)
            top = m_ref[here]
            for n, (p, k, part) in enumerate(pieces):
                j = p * 2 + k
                lane = part * (rows // 2)
                base = jnp.where(j <= ctx, j * rows + lane, -TOO_FAR)
                allowed = first_ref[...] <= base + lane_iota
                if diagonal:
                    local = lax.broadcasted_iota(jnp.int32, (block_rows, 128), 0)
                    ahead = lane + lax.broadcasted_iota(jnp.int32, (block_rows, 128), 1)
                    allowed = allowed & (ahead <= lax.rem(local, rows))
                one = jnp.where(allowed, s[:, n * 128 : (n + 1) * 128], NEG)
                s_ref[j, here, lane : lane + 128] = one
                top = jnp.maximum(top, one)
            m_ref[here] = top
            return carry

        lax.fori_loop(0, groups, one_group, 0)

    def near_tile(turn, k):
        below, above = block(0, origin[0]), block(0, origin[1])

        @pl.when((below * 2 + k < ctx) | (above * 2 + k < ctx))
        def _():
            scores(((below, k, turn), (above, k, 1 - turn)), False)

    def tiles(plane, r, count, k):
        def one(i, carry):
            p = planes[plane] + lax.rem(x + r + 2 * i, 4)

            @pl.when(p * 2 + k < ctx)
            def _():
                scores(((p, k, 0), (p, k, 1)), True)

            return carry

        lax.fori_loop(0, count, one, 0)

    scores(((mine, core, 0), (mine, core, 1)), True, True)
    from_sibling(0, 0)
    tiles(0, 0, 1, 1 - core)
    strips_onward()
    own_onward()
    near_tile(0, core)
    y_step2(0)
    half_from_sibling(0)
    near_tile(0, 1 - core)
    own_near()
    strips_far()
    near_tile(1, core)
    y_step2(1)
    y_step2(3)
    y_finish(0)
    half_from_sibling(1)
    near_tile(1, 1 - core)
    own_far()
    y_step2(2)
    tiles(1, 0, 1, core)
    tiles(0, 2, 1, core)
    y_finish(1)
    y_finish(3)
    from_sibling(1, 0)
    tiles(1, 0, 1, 1 - core)
    y_finish(2)
    tiles(1, 1, 2, core)
    from_sibling(0, 2)
    tiles(0, 2, 1, 1 - core)
    from_sibling(1, 1)
    from_sibling(1, 3)
    tiles(1, 1, 2, 1 - core)
    tiles(1, 2, 1, core)
    from_sibling(1, 2)
    tiles(1, 2, 1, 1 - core)

    @pl.when(core == 0)
    def _():
        s_ref[ctx + 1] = jnp.full(s_ref.shape[1:], NEG, jnp.float32)

    loads[4].wait()

    def context_of(g, carry):
        here = pl.ds(pl.multiple_of(g * block_rows, block_rows), block_rows)
        m = jnp.max(m_ref[here], axis=1, keepdims=True)
        m_ref[here] = jnp.broadcast_to(m, (block_rows, 128))
        l_ref[...] = jnp.zeros_like(l_ref)
        acc_ref[...] = jnp.zeros_like(acc_ref)

        def weigh(p, carry):
            top = m_ref[here]
            weights = []
            total = l_ref[...]
            for k in range(2):
                for lane in range(0, rows, 128):
                    s = s_ref[2 * p + k, here, lane : lane + 128]
                    w = jnp.exp2((s - top) * EXP_SCALE)
                    total = total + w
                    weights.append(w.astype(jnp.bfloat16))
            l_ref[...] = total
            values = keys_ref[p, :, :, :LAT].reshape(2 * rows, LAT)
            acc_ref[...] += jnp.dot(
                jnp.concatenate(weights, axis=1), values, preferred_element_type=jnp.float32
            )
            return carry

        lax.fori_loop(0, ctx // 2 + 1, weigh, 0)
        inverse = 1.0 / jnp.sum(l_ref[...], axis=1, keepdims=True)
        context = (acc_ref[...] * inverse).astype(jnp.bfloat16)
        for i in range(GROUP):
            h = g * GROUP + i
            one = jnp.dot(
                context[i * rows : (i + 1) * rows], uv_ref[h], preferred_element_type=jnp.float32
            )
            out_ref[:, pl.ds(pl.multiple_of(h * VDIM, VDIM), VDIM)] = one.astype(jnp.bfloat16)
        return carry

    lax.fori_loop(0, groups, context_of, 0)
    for one in pending:
        one.wait_send()


def attend(doc_lengths, by_head, latents, scale_row, w_uk, w_uv):
    heads, _, rows = by_head.shape
    width = latents.shape[0]
    dma = pltpu.SemaphoreType.DMA
    vmem = pltpu.VMEM
    outside = pl.BlockSpec(memory_space=pl.ANY)
    whole = pl.BlockSpec(memory_space=pltpu.VMEM)
    block_rows = GROUP * rows
    return pl.pallas_call(
        attend_kernel,
        out_shape=jax.ShapeDtypeStruct((rows, heads * VDIM), jnp.bfloat16),
        in_specs=[outside] * 6,
        out_specs=whole,
        scratch_shapes=[
            pltpu.SMEM(doc_lengths.shape, jnp.int32),
            vmem(by_head.shape, by_head.dtype),
            vmem(latents.shape, latents.dtype),
            vmem(scale_row.shape, scale_row.dtype),
            vmem(w_uk.shape, w_uk.dtype),
            vmem(w_uv.shape, w_uv.dtype),
            vmem((8, 2, rows, width), jnp.bfloat16),
            vmem((heads, rows, width), jnp.bfloat16),
            vmem((16, heads * rows, rows), jnp.float32),
            vmem((heads * rows, 128), jnp.float32),
            vmem((block_rows, 128), jnp.float32),
            vmem((block_rows, LAT), jnp.float32),
            vmem((block_rows, 128), jnp.int32),
            dma((6,)),
            dma((1,)), dma((1,)),
            dma((4,)), dma((4,)),
            dma((2,)), dma((2,)),
            dma((2,)), dma((2,)),
            dma((2,)), dma((2,)),
            dma((8,)), dma((8,)),
            dma((8,)), dma((8,)),
            dma((8,)), dma((8,)),
            dma((4,)), dma((4,)),
        ],
        compiler_params=pltpu.CompilerParams(
            collective_id=1, has_side_effects=True, vmem_limit_bytes=61 << 20
        ),
        name="attend",
    )(doc_lengths, by_head, latents, scale_row, w_uk, w_uv)


def reduce_kernel(
    x_hbm, w_ref, out_ref, x_ref, x_sem, wbuf, own, zrecv, y1recv, y2recv, ysecond1, ysecond2, zlast,
    wsem, zsend, zgot, y1send, y1got, y2send, y2got, s1send, s1got, s2send, s2got, lsend, lgot,
):
    cols = out_ref.shape[1]
    half = out_ref.shape[0] // 2
    quarter = half // 2
    me = lax.axis_index("head")
    y = lax.rem(me, 4)
    z = me // 4
    up = z * 4 + lax.rem(y + 1, 4)
    down = z * 4 + lax.rem(y + 3, 4)
    across = (1 - z) * 4 + y
    blocks = ((2, 0), (2, 1), (1, 0), (3, 0), (1, 1), (3, 1), (0, 0), (0, 1))
    slot = {key: k for k, key in enumerate(blocks)}
    first = pl.ds(0, half)
    second = pl.ds(half, half)

    def fetch(k):
        shift, mine = blocks[k]
        plane = z if mine else 1 - z
        start = pl.multiple_of((plane * 4 + lax.rem(y + shift, 4)) * cols, 128)
        return pltpu.make_async_copy(w_ref.at[:, pl.ds(start, cols)], wbuf.at[k], wsem.at[k])

    def send(src, dst, ssem, rsem, target):
        return pltpu.make_async_remote_copy(
            src_ref=src, dst_ref=dst, send_sem=ssem, recv_sem=rsem,
            device_id={"head": target}, device_id_type=MESH,
        )

    load = pltpu.make_async_copy(x_hbm, x_ref, x_sem.at[0])
    load.start()
    for k in range(2):
        fetch(k).start()
    barrier = pltpu.get_barrier_semaphore()
    for target in (up, down, across):
        pl.semaphore_signal(barrier, inc=1, device_id={"head": target}, device_id_type=MESH)
    load.wait()

    pending = []

    def go(copy):
        copy.start()
        pending.append(copy)

    def across_copy(i, k):
        return send(own.at[k, first], zrecv.at[i], zsend.at[i], zgot.at[i], across)

    def step1(k, base, buf, ssem, rsem, i):
        go(send(own.at[k, pl.ds(base, quarter)], buf.at[i], ssem.at[i], rsem.at[i], up))
        go(
            send(
                own.at[k, pl.ds(base + quarter, quarter)],
                buf.at[i + 1], ssem.at[i + 1], rsem.at[i + 1], down,
            )
        )

    across_order = (2, 1, 3, 0)
    across_copies = {}

    def compute(k):
        fetch(k).wait()
        if k + 2 < 8:
            fetch(k + 2).start()
        own[k] = jnp.dot(x_ref[...], wbuf[k], preferred_element_type=jnp.float32).astype(
            jnp.bfloat16
        )
        if k == 0:
            pl.semaphore_wait(barrier, 3)
        shift, mine = blocks[k]
        if not mine:
            i = across_order.index(shift)
            across_copies[i] = across_copy(i, k)
            go(across_copies[i])
        if shift == 2:
            step1(k, half, y1recv, y1send, y1got, 2 * mine)

    def add_rows(k, rows, *terms):
        total = own[k, rows].astype(jnp.float32)
        for term in terms:
            total = total + term.astype(jnp.float32)
        return total

    copies = {}

    def y_first_step2(mine):
        for side, (shift, target, offset) in enumerate(((1, up, 0), (3, down, quarter))):
            k = slot[(shift, mine)]
            i = 2 * mine + side
            rows = pl.ds(half + offset, quarter)
            send(
                own.at[0, pl.ds(0, quarter)], y1recv.at[i], y1send.at[i], y1got.at[i], target
            ).wait_recv()
            own[k, rows] = add_rows(k, rows, y1recv[i]).astype(jnp.bfloat16)
            go(send(own.at[k, second], y2recv.at[i], y2send.at[i], y2got.at[i], target))

    def got(buf, i, ssem, rsem, rows):
        send(own.at[0, pl.ds(0, rows)], buf.at[i], ssem.at[i], rsem.at[i], across).wait_recv()

    for k in range(6):
        compute(k)
    y_first_step2(0)
    for k in range(6, 8):
        compute(k)
    y_first_step2(1)

    got(zrecv, 0, zsend, zgot, half)
    k = slot[(2, 1)]
    own[k, first] = add_rows(k, first, zrecv[0]).astype(jnp.bfloat16)
    step1(k, 0, ysecond1, s1send, s1got, 0)

    got(y2recv, 0, y2send, y2got, half)
    got(y2recv, 1, y2send, y2got, half)
    k = slot[(0, 0)]
    own[k, second] = add_rows(k, second, y2recv[0], y2recv[1]).astype(jnp.bfloat16)
    go(send(own.at[k, second], zlast.at[0], lsend.at[0], lgot.at[0], across))

    for side, (shift, target, offset) in enumerate(((1, up, 0), (3, down, quarter))):
        k = slot[(shift, 1)]
        got(zrecv, 1 + side, zsend, zgot, half)
        got(ysecond1, side, s1send, s1got, quarter)
        own[k, first] = add_rows(k, first, zrecv[1 + side]).astype(jnp.bfloat16)
        rows = pl.ds(offset, quarter)
        own[k, rows] = add_rows(k, rows, ysecond1[side]).astype(jnp.bfloat16)
        go(send(own.at[k, first], ysecond2.at[side], s2send.at[side], s2got.at[side], target))

    k = slot[(0, 1)]
    got(y2recv, 2, y2send, y2got, half)
    got(y2recv, 3, y2send, y2got, half)
    got(zlast, 0, lsend, lgot, half)
    out_ref[second] = add_rows(k, second, y2recv[2], y2recv[3], zlast[0]).astype(jnp.bfloat16)
    got(zrecv, 3, zsend, zgot, half)
    got(ysecond2, 0, s2send, s2got, half)
    got(ysecond2, 1, s2send, s2got, half)
    out_ref[first] = add_rows(k, first, zrecv[3], ysecond2[0], ysecond2[1]).astype(jnp.bfloat16)
    for copy in pending:
        copy.wait_send()


def project_and_reduce(head_out, w_o):
    rows, inner = head_out.shape
    cols = w_o.shape[1] // 8
    half = rows // 2
    dma = pltpu.SemaphoreType.DMA
    return pl.pallas_call(
        reduce_kernel,
        out_shape=jax.ShapeDtypeStruct((rows, cols), jnp.bfloat16),
        in_specs=[pl.BlockSpec(memory_space=pltpu.HBM)] * 2,
        out_specs=pl.BlockSpec(memory_space=pltpu.VMEM),
        scratch_shapes=[
            pltpu.VMEM((rows, inner), jnp.bfloat16),
            dma((1,)),
            pltpu.VMEM((8, inner, cols), jnp.bfloat16),
            pltpu.VMEM((8, rows, cols), jnp.bfloat16),
            pltpu.VMEM((4, half, cols), jnp.bfloat16),
            pltpu.VMEM((4, half // 2, cols), jnp.bfloat16),
            pltpu.VMEM((4, half, cols), jnp.bfloat16),
            pltpu.VMEM((2, half // 2, cols), jnp.bfloat16),
            pltpu.VMEM((2, half, cols), jnp.bfloat16),
            pltpu.VMEM((1, half, cols), jnp.bfloat16),
            dma((8,)),
            dma((4,)), dma((4,)),
            dma((4,)), dma((4,)),
            dma((4,)), dma((4,)),
            dma((2,)), dma((2,)),
            dma((2,)), dma((2,)),
            dma((1,)), dma((1,)),
        ],
        compiler_params=pltpu.CompilerParams(
            collective_id=0, has_side_effects=True, vmem_limit_bytes=62 << 20
        ),
        name="project_and_reduce",
    )(head_out, w_o)


def shards(query, latents, lat_scale, doc_lengths, w_uk, w_uv, w_o):
    by_head = jnp.transpose(query, (1, 2, 0))
    head_out = attend(doc_lengths, by_head, latents.T, lat_scale.reshape(1, -1), w_uk, w_uv)
    return project_and_reduce(head_out, w_o)


def solution(mesh):
    placed = (
        P("ctx", "head", None),
        P("ctx", None),
        P("ctx"),
        P(),
        P("head", None, None),
        P("head", None, None),
        P("head", None),
    )
    return jax.shard_map(
        shards, mesh=mesh, in_specs=placed, out_specs=P("ctx", "head"), check_vma=False
    )
```

```python
import jax
import jax.numpy as jnp
from jax import lax
from jax.experimental import pallas as pl
from jax.experimental.pallas import tpu as pltpu
from jax.sharding import PartitionSpec as P

LAT = 512
NOPE = 128
QDIM = 192
VDIM = 128
GROUP = 8
NEG = -1e30
TOO_FAR = 1 << 20
MESH = pl.DeviceIdType.MESH
EXP_SCALE = float(QDIM) ** -0.5 * 1.4426950408889634


def attend_kernel(
    lens_hbm, q_hbm, latents_hbm, scale_hbm, uk_hbm, uv_hbm, out_ref,
    lens_ref, q_ref, latents_ref, scale_ref, uk_ref, uv_ref,
    keys_ref, qf_ref, s_ref, m_ref, l_ref, acc_ref, first_ref, load_sem,
    zsend, zgot, x1send, x1got, x2send, x2got, s1send, s1got, s2send, s2got,
    y1send, y1got, y2send, y2got, csend, cgot, hsend, hgot,
):
    rows = latents_ref.shape[1]
    heads = q_ref.shape[0]
    block_rows = GROUP * rows
    groups = heads // GROUP
    ctx = lax.axis_index("ctx")
    head = lax.axis_index("head")
    core = lax.rem(ctx, 2)
    x = lax.rem(ctx // 2, 4)
    hi = ctx // 8
    y = lax.rem(head, 4)
    lo = head // 4
    x_up, x_down, x_far = lax.rem(x + 1, 4), lax.rem(x + 3, 4), lax.rem(x + 2, 4)
    y_up, y_down, y_far = lax.rem(y + 1, 4), lax.rem(y + 3, 4), lax.rem(y + 2, 4)
    planes = (hi * 4, (1 - hi) * 4)
    around = (x, x_up, x_far, x_down)

    loads = [
        pltpu.make_async_copy(src, dst, load_sem.at[i])
        for i, (src, dst) in enumerate(
            (
                (latents_hbm, latents_ref),
                (scale_hbm, scale_ref),
                (uk_hbm, uk_ref),
                (lens_hbm, lens_ref),
                (uv_hbm, uv_ref),
                (q_hbm, q_ref),
            )
        )
    ]
    for load in loads:
        load.start()

    def place(a, b, c, d, e):
        return {"ctx": a * 8 + b * 2 + c, "head": d * 4 + e}

    to_x = (place(hi, x_up, core, lo, y), place(hi, x_down, core, lo, y))
    to_y = (place(hi, x, core, lo, y_up), place(hi, x, core, lo, y_down))
    to_z = place(1 - hi, x, core, 1 - lo, y)
    to_core = place(hi, x, 1 - core, lo, y)

    def copy(src, dst, ssem, rsem, target):
        return pltpu.make_async_remote_copy(
            src_ref=src, dst_ref=dst, send_sem=ssem, recv_sem=rsem,
            device_id=target, device_id_type=MESH,
        )

    pending = []

    def go(ref, ssem, rsem, target):
        one = copy(ref, ref, ssem, rsem, target)
        one.start()
        pending.append(one)

    def got(ref, ssem, rsem):
        copy(ref, ref, ssem, rsem, to_core).wait_recv()

    barrier = pltpu.get_barrier_semaphore()
    for target in (*to_x, *to_y, to_z, to_core):
        pl.semaphore_signal(barrier, inc=1, device_id=target, device_id_type=MESH)

    def block(plane, r):
        return planes[plane] + around[r]

    loads[0].wait()
    loads[1].wait()
    mine = block(0, 0)
    latent = latents_ref[...].astype(jnp.float32)
    keys_ref[mine, core, :, :LAT] = (latent[:LAT] * scale_ref[...]).T.astype(jnp.bfloat16)
    keys_ref[mine, core, :, LAT:] = latent[LAT:].T.astype(jnp.bfloat16)

    pl.semaphore_wait(barrier, 6)

    parts = (pl.ds(0, rows // 2), pl.ds(rows // 2, rows // 2))
    width = rows // 4

    def strip(index):
        return pl.ds(pl.multiple_of(index * width, 16), width)

    def strip_half(index, which):
        return pl.ds(pl.multiple_of(index * width + which * (width // 2), 16), width // 2)

    def at(plane, r, part):
        return keys_ref.at[block(plane, r), core, part]

    def to_sibling(plane, r):
        i = plane * 4 + r
        go(keys_ref.at[block(plane, r), core], csend.at[i], cgot.at[i], to_core)

    def from_sibling(plane, r):
        i = plane * 4 + r
        got(keys_ref.at[block(plane, r), 1 - core], csend.at[i], cgot.at[i])

    origin = (3, 1)

    def own_first():
        for d in range(2):
            go(at(0, 0, parts[d]), x1send.at[d], x1got.at[d], to_x[d])

    def own_second():
        for d in range(2):
            go(at(0, 0, parts[1 - d]), x1send.at[2 + d], x1got.at[2 + d], to_x[d])

    def near(turn, d):
        return at(0, origin[d], parts[d if turn == 0 else 1 - d])

    def half_to_sibling(turn):
        for d in range(2):
            i = turn * 2 + d
            go(near(turn, d), hsend.at[i], hgot.at[i], to_core)

    def half_from_sibling(turn):
        for d in range(2):
            i = turn * 2 + d
            ref = keys_ref.at[block(0, origin[d]), 1 - core, parts[d if turn == 0 else 1 - d]]
            got(ref, hsend.at[i], hgot.at[i])

    def own_onward():
        for d in range(2):
            got(near(0, d), x1send.at[d], x1got.at[d])
            go(near(0, d), x2send.at[d], x2got.at[d], to_x[d])
        half_to_sibling(0)

    def own_near():
        for d in range(2):
            got(near(1, d), x1send.at[2 + d], x1got.at[2 + d])
        half_to_sibling(1)

    def own_far():
        for d in range(2):
            got(at(0, 2, parts[d]), x2send.at[d], x2got.at[d])
        to_sibling(0, 2)

    def y_step1(r):
        for d in range(2):
            i = r * 2 + d
            go(at(1, r, strip(y)), y1send.at[i], y1got.at[i], to_y[d])

    def from_z():
        got(at(1, 0, strip(y)), zsend.at[0], zgot.at[0])
        for d in range(2):
            go(at(1, 0, strip(y)), s1send.at[d], s1got.at[d], to_x[d])
        y_step1(0)

    def strips_onward():
        for d in range(2):
            got(at(1, origin[d], strip(y)), s1send.at[d], s1got.at[d])
            go(at(1, origin[d], strip_half(y, d)), s2send.at[d], s2got.at[d], to_x[d])
        y_step1(1)
        y_step1(3)

    def strips_far():
        for d in range(2):
            got(at(1, 2, strip_half(y, d)), s2send.at[d], s2got.at[d])
        y_step1(2)

    def y_step2(r):
        for d, source in enumerate((y_down, y_up)):
            i = r * 2 + d
            got(at(1, r, strip(source)), y1send.at[i], y1got.at[i])
            go(at(1, r, strip_half(source, d)), y2send.at[i], y2got.at[i], to_y[d])

    def y_finish(r):
        for d in range(2):
            i = r * 2 + d
            got(at(1, r, strip_half(y_far, d)), y2send.at[i], y2got.at[i])
        to_sibling(1, r)

    def queries():
        for h in range(heads):
            q = q_ref[h].astype(jnp.float32).T.astype(jnp.bfloat16)
            lat = jnp.dot(q[:, :NOPE], uk_ref[h], preferred_element_type=jnp.float32)
            qf_ref[h, :, :LAT] = lat.astype(jnp.bfloat16)
            qf_ref[h, :, LAT:] = q[:, NOPE:]

    go(at(0, 0, strip(y)), zsend.at[0], zgot.at[0], to_z)
    own_first()
    to_sibling(0, 0)
    loads[2].wait()
    loads[5].wait()
    queries()
    from_z()
    own_second()

    loads[3].wait()
    t0 = ctx * rows
    qpos = t0 + lax.broadcasted_iota(jnp.int32, (rows, 128), 0)
    first = jnp.zeros_like(qpos)
    end = jnp.int32(0)
    for k in range(lens_ref.shape[0]):
        end = end + lens_ref[k]
        first = jnp.where(qpos >= end, end, first)
    first_ref[...] = jnp.concatenate([first] * GROUP, axis=0)
    m_ref[...] = jnp.full_like(m_ref, NEG)

    lane_iota = lax.broadcasted_iota(jnp.int32, (1, 128), 1)

    def scores(pieces, whole, diagonal=False):
        def one_group(g, carry):
            q = qf_ref[pl.ds(g * GROUP, GROUP)].reshape(block_rows, -1)
            if whole:
                keys = keys_ref[pieces[0][0], pieces[0][1]]
            else:
                keys = jnp.concatenate([keys_ref[p, k, parts[part]] for p, k, part in pieces], axis=0)
            s = lax.dot_general(
                q, keys, (((1,), (1,)), ((), ())), preferred_element_type=jnp.float32
            )
            here = pl.ds(pl.multiple_of(g * block_rows, block_rows), block_rows)
            top = m_ref[here]
            for n, (p, k, part) in enumerate(pieces):
                j = p * 2 + k
                lane = part * (rows // 2)
                base = jnp.where(j <= ctx, j * rows + lane, -TOO_FAR)
                allowed = first_ref[...] <= base + lane_iota
                if diagonal:
                    local = lax.broadcasted_iota(jnp.int32, (block_rows, 128), 0)
                    ahead = lane + lax.broadcasted_iota(jnp.int32, (block_rows, 128), 1)
                    allowed = allowed & (ahead <= lax.rem(local, rows))
                one = jnp.where(allowed, s[:, n * 128 : (n + 1) * 128], NEG)
                s_ref[j, here, lane : lane + 128] = one
                top = jnp.maximum(top, one)
            m_ref[here] = top
            return carry

        lax.fori_loop(0, groups, one_group, 0)

    def near_tile(turn, k):
        below, above = block(0, origin[0]), block(0, origin[1])

        @pl.when((below * 2 + k < ctx) | (above * 2 + k < ctx))
        def _():
            scores(((below, k, turn), (above, k, 1 - turn)), False)

    def tiles(plane, r, count, k):
        def one(i, carry):
            p = planes[plane] + lax.rem(x + r + 2 * i, 4)

            @pl.when(p * 2 + k < ctx)
            def _():
                scores(((p, k, 0), (p, k, 1)), True)

            return carry

        lax.fori_loop(0, count, one, 0)

    scores(((mine, core, 0), (mine, core, 1)), True, True)
    from_sibling(0, 0)
    tiles(0, 0, 1, 1 - core)
    strips_onward()
    own_onward()
    near_tile(0, core)
    y_step2(0)
    half_from_sibling(0)
    near_tile(0, 1 - core)
    own_near()
    strips_far()
    near_tile(1, core)
    y_step2(1)
    y_step2(3)
    y_finish(0)
    half_from_sibling(1)
    near_tile(1, 1 - core)
    own_far()
    y_step2(2)
    tiles(1, 0, 1, core)
    tiles(0, 2, 1, core)
    y_finish(1)
    y_finish(3)
    from_sibling(1, 0)
    tiles(1, 0, 1, 1 - core)
    y_finish(2)
    tiles(1, 1, 2, core)
    from_sibling(0, 2)
    tiles(0, 2, 1, 1 - core)
    from_sibling(1, 1)
    from_sibling(1, 3)
    tiles(1, 1, 2, 1 - core)
    tiles(1, 2, 1, core)
    from_sibling(1, 2)
    tiles(1, 2, 1, 1 - core)

    @pl.when(core == 0)
    def _():
        s_ref[ctx + 1] = jnp.full(s_ref.shape[1:], NEG, jnp.float32)

    loads[4].wait()

    def context_of(g, carry):
        here = pl.ds(pl.multiple_of(g * block_rows, block_rows), block_rows)
        m = jnp.max(m_ref[here], axis=1, keepdims=True)
        m_ref[here] = jnp.broadcast_to(m, (block_rows, 128))
        l_ref[...] = jnp.zeros_like(l_ref)
        acc_ref[...] = jnp.zeros_like(acc_ref)

        def weigh(p, carry):
            top = m_ref[here]
            weights = []
            total = l_ref[...]
            for k in range(2):
                for lane in range(0, rows, 128):
                    s = s_ref[2 * p + k, here, lane : lane + 128]
                    w = jnp.exp2((s - top) * EXP_SCALE)
                    total = total + w
                    weights.append(w.astype(jnp.bfloat16))
            l_ref[...] = total
            values = keys_ref[p, :, :, :LAT].reshape(2 * rows, LAT)
            acc_ref[...] += jnp.dot(
                jnp.concatenate(weights, axis=1), values, preferred_element_type=jnp.float32
            )
            return carry

        lax.fori_loop(0, ctx // 2 + 1, weigh, 0)
        inverse = 1.0 / jnp.sum(l_ref[...], axis=1, keepdims=True)
        context = (acc_ref[...] * inverse).astype(jnp.bfloat16)
        for i in range(GROUP):
            h = g * GROUP + i
            one = jnp.dot(
                context[i * rows : (i + 1) * rows], uv_ref[h], preferred_element_type=jnp.float32
            )
            out_ref[:, pl.ds(pl.multiple_of(h * VDIM, VDIM), VDIM)] = one.astype(jnp.bfloat16)
        return carry

    lax.fori_loop(0, groups, context_of, 0)
    for one in pending:
        one.wait_send()


def attend(doc_lengths, by_head, latents, scale_row, w_uk, w_uv):
    heads, _, rows = by_head.shape
    width = latents.shape[0]
    dma = pltpu.SemaphoreType.DMA
    vmem = pltpu.VMEM
    outside = pl.BlockSpec(memory_space=pl.ANY)
    whole = pl.BlockSpec(memory_space=pltpu.VMEM)
    block_rows = GROUP * rows
    return pl.pallas_call(
        attend_kernel,
        out_shape=jax.ShapeDtypeStruct((rows, heads * VDIM), jnp.bfloat16),
        in_specs=[outside] * 6,
        out_specs=whole,
        scratch_shapes=[
            pltpu.SMEM(doc_lengths.shape, jnp.int32),
            vmem(by_head.shape, by_head.dtype),
            vmem(latents.shape, latents.dtype),
            vmem(scale_row.shape, scale_row.dtype),
            vmem(w_uk.shape, w_uk.dtype),
            vmem(w_uv.shape, w_uv.dtype),
            vmem((8, 2, rows, width), jnp.bfloat16),
            vmem((heads, rows, width), jnp.bfloat16),
            vmem((16, heads * rows, rows), jnp.float32),
            vmem((heads * rows, 128), jnp.float32),
            vmem((block_rows, 128), jnp.float32),
            vmem((block_rows, LAT), jnp.float32),
            vmem((block_rows, 128), jnp.int32),
            dma((6,)),
            dma((1,)), dma((1,)),
            dma((4,)), dma((4,)),
            dma((2,)), dma((2,)),
            dma((2,)), dma((2,)),
            dma((2,)), dma((2,)),
            dma((8,)), dma((8,)),
            dma((8,)), dma((8,)),
            dma((8,)), dma((8,)),
            dma((4,)), dma((4,)),
        ],
        compiler_params=pltpu.CompilerParams(
            collective_id=1, has_side_effects=True, vmem_limit_bytes=61 << 20
        ),
        name="attend",
    )(doc_lengths, by_head, latents, scale_row, w_uk, w_uv)


def reduce_kernel(
    x_hbm, w_ref, out_ref, x_ref, x_sem, wbuf, own, zrecv, y1recv, y2recv, ysecond1, ysecond2, zlast,
    wsem, zsend, zgot, y1send, y1got, y2send, y2got, s1send, s1got, s2send, s2got, lsend, lgot,
):
    cols = out_ref.shape[1]
    half = out_ref.shape[0] // 2
    quarter = half // 2
    me = lax.axis_index("head")
    y = lax.rem(me, 4)
    z = me // 4
    up = z * 4 + lax.rem(y + 1, 4)
    down = z * 4 + lax.rem(y + 3, 4)
    across = (1 - z) * 4 + y
    blocks = ((2, 0), (2, 1), (1, 0), (3, 0), (1, 1), (3, 1), (0, 0), (0, 1))
    slot = {key: k for k, key in enumerate(blocks)}
    first = pl.ds(0, half)
    second = pl.ds(half, half)

    def fetch(k):
        shift, mine = blocks[k]
        plane = z if mine else 1 - z
        start = pl.multiple_of((plane * 4 + lax.rem(y + shift, 4)) * cols, 128)
        return pltpu.make_async_copy(w_ref.at[:, pl.ds(start, cols)], wbuf.at[k], wsem.at[k])

    def send(src, dst, ssem, rsem, target):
        return pltpu.make_async_remote_copy(
            src_ref=src, dst_ref=dst, send_sem=ssem, recv_sem=rsem,
            device_id={"head": target}, device_id_type=MESH,
        )

    load = pltpu.make_async_copy(x_hbm, x_ref, x_sem.at[0])
    load.start()
    for k in range(2):
        fetch(k).start()
    barrier = pltpu.get_barrier_semaphore()
    for target in (up, down, across):
        pl.semaphore_signal(barrier, inc=1, device_id={"head": target}, device_id_type=MESH)
    load.wait()

    pending = []

    def go(copy):
        copy.start()
        pending.append(copy)

    def across_copy(i, k):
        return send(own.at[k, first], zrecv.at[i], zsend.at[i], zgot.at[i], across)

    def step1(k, base, buf, ssem, rsem, i):
        go(send(own.at[k, pl.ds(base, quarter)], buf.at[i], ssem.at[i], rsem.at[i], up))
        go(
            send(
                own.at[k, pl.ds(base + quarter, quarter)],
                buf.at[i + 1], ssem.at[i + 1], rsem.at[i + 1], down,
            )
        )

    across_order = (2, 1, 3, 0)
    across_copies = {}

    def compute(k):
        fetch(k).wait()
        if k + 2 < 8:
            fetch(k + 2).start()
        own[k] = jnp.dot(x_ref[...], wbuf[k], preferred_element_type=jnp.float32).astype(
            jnp.bfloat16
        )
        if k == 0:
            pl.semaphore_wait(barrier, 3)
        shift, mine = blocks[k]
        if not mine:
            i = across_order.index(shift)
            across_copies[i] = across_copy(i, k)
            go(across_copies[i])
        if shift == 2:
            step1(k, half, y1recv, y1send, y1got, 2 * mine)

    def add_rows(k, rows, *terms):
        total = own[k, rows].astype(jnp.float32)
        for term in terms:
            total = total + term.astype(jnp.float32)
        return total

    copies = {}

    def y_first_step2(mine):
        for side, (shift, target, offset) in enumerate(((1, up, 0), (3, down, quarter))):
            k = slot[(shift, mine)]
            i = 2 * mine + side
            rows = pl.ds(half + offset, quarter)
            send(
                own.at[0, pl.ds(0, quarter)], y1recv.at[i], y1send.at[i], y1got.at[i], target
            ).wait_recv()
            own[k, rows] = add_rows(k, rows, y1recv[i]).astype(jnp.bfloat16)
            go(send(own.at[k, second], y2recv.at[i], y2send.at[i], y2got.at[i], target))

    def got(buf, i, ssem, rsem, rows):
        send(own.at[0, pl.ds(0, rows)], buf.at[i], ssem.at[i], rsem.at[i], across).wait_recv()

    for k in range(6):
        compute(k)
    y_first_step2(0)
    compute(6)

    got(zrecv, 0, zsend, zgot, half)
    k = slot[(2, 1)]
    own[k, first] = add_rows(k, first, zrecv[0]).astype(jnp.bfloat16)
    step1(k, 0, ysecond1, s1send, s1got, 0)

    compute(7)
    y_first_step2(1)

    got(y2recv, 0, y2send, y2got, half)
    got(y2recv, 1, y2send, y2got, half)
    k = slot[(0, 0)]
    own[k, second] = add_rows(k, second, y2recv[0], y2recv[1]).astype(jnp.bfloat16)
    go(send(own.at[k, second], zlast.at[0], lsend.at[0], lgot.at[0], across))

    for side, (shift, target, offset) in enumerate(((1, up, 0), (3, down, quarter))):
        k = slot[(shift, 1)]
        got(zrecv, 1 + side, zsend, zgot, half)
        got(ysecond1, side, s1send, s1got, quarter)
        own[k, first] = add_rows(k, first, zrecv[1 + side]).astype(jnp.bfloat16)
        rows = pl.ds(offset, quarter)
        own[k, rows] = add_rows(k, rows, ysecond1[side]).astype(jnp.bfloat16)
        go(send(own.at[k, first], ysecond2.at[side], s2send.at[side], s2got.at[side], target))

    k = slot[(0, 1)]
    got(y2recv, 2, y2send, y2got, half)
    got(y2recv, 3, y2send, y2got, half)
    got(zlast, 0, lsend, lgot, half)
    out_ref[second] = add_rows(k, second, y2recv[2], y2recv[3], zlast[0]).astype(jnp.bfloat16)
    got(zrecv, 3, zsend, zgot, half)
    got(ysecond2, 0, s2send, s2got, half)
    got(ysecond2, 1, s2send, s2got, half)
    out_ref[first] = add_rows(k, first, zrecv[3], ysecond2[0], ysecond2[1]).astype(jnp.bfloat16)
    for copy in pending:
        copy.wait_send()


def project_and_reduce(head_out, w_o):
    rows, inner = head_out.shape
    cols = w_o.shape[1] // 8
    half = rows // 2
    dma = pltpu.SemaphoreType.DMA
    return pl.pallas_call(
        reduce_kernel,
        out_shape=jax.ShapeDtypeStruct((rows, cols), jnp.bfloat16),
        in_specs=[pl.BlockSpec(memory_space=pltpu.HBM)] * 2,
        out_specs=pl.BlockSpec(memory_space=pltpu.VMEM),
        scratch_shapes=[
            pltpu.VMEM((rows, inner), jnp.bfloat16),
            dma((1,)),
            pltpu.VMEM((8, inner, cols), jnp.bfloat16),
            pltpu.VMEM((8, rows, cols), jnp.bfloat16),
            pltpu.VMEM((4, half, cols), jnp.bfloat16),
            pltpu.VMEM((4, half // 2, cols), jnp.bfloat16),
            pltpu.VMEM((4, half, cols), jnp.bfloat16),
            pltpu.VMEM((2, half // 2, cols), jnp.bfloat16),
            pltpu.VMEM((2, half, cols), jnp.bfloat16),
            pltpu.VMEM((1, half, cols), jnp.bfloat16),
            dma((8,)),
            dma((4,)), dma((4,)),
            dma((4,)), dma((4,)),
            dma((4,)), dma((4,)),
            dma((2,)), dma((2,)),
            dma((2,)), dma((2,)),
            dma((1,)), dma((1,)),
        ],
        compiler_params=pltpu.CompilerParams(
            collective_id=0, has_side_effects=True, vmem_limit_bytes=62 << 20
        ),
        name="project_and_reduce",
    )(head_out, w_o)


def shards(query, latents, lat_scale, doc_lengths, w_uk, w_uv, w_o):
    by_head = jnp.transpose(query, (1, 2, 0))
    head_out = attend(doc_lengths, by_head, latents.T, lat_scale.reshape(1, -1), w_uk, w_uv)
    return project_and_reduce(head_out, w_o)


def solution(mesh):
    placed = (
        P("ctx", "head", None),
        P("ctx", None),
        P("ctx"),
        P(),
        P("head", None, None),
        P("head", None, None),
        P("head", None),
    )
    return jax.shard_map(
        shards, mesh=mesh, in_specs=placed, out_specs=P("ctx", "head"), check_vma=False
    )
```

```python
import jax
import jax.numpy as jnp
from jax import lax
from jax.experimental import pallas as pl
from jax.experimental.pallas import tpu as pltpu
from jax.sharding import PartitionSpec as P

LAT = 512
NOPE = 128
QDIM = 192
VDIM = 128
GROUP = 8
NEG = -1e30
TOO_FAR = 1 << 20
MESH = pl.DeviceIdType.MESH
EXP_SCALE = float(QDIM) ** -0.5 * 1.4426950408889634


def attend_kernel(
    lens_hbm, q_hbm, latents_hbm, scale_hbm, uk_hbm, uv_hbm, out_ref,
    lens_ref, q_ref, latents_ref, scale_ref, uk_ref, uv_ref,
    keys_ref, qf_ref, s_ref, m_ref, l_ref, acc_ref, first_ref, load_sem,
    zsend, zgot, x1send, x1got, x2send, x2got, s1send, s1got, s2send, s2got,
    y1send, y1got, y2send, y2got, csend, cgot, hsend, hgot,
):
    rows = latents_ref.shape[1]
    heads = q_ref.shape[0]
    block_rows = GROUP * rows
    groups = heads // GROUP
    ctx = lax.axis_index("ctx")
    head = lax.axis_index("head")
    core = lax.rem(ctx, 2)
    x = lax.rem(ctx // 2, 4)
    hi = ctx // 8
    y = lax.rem(head, 4)
    lo = head // 4
    x_up, x_down, x_far = lax.rem(x + 1, 4), lax.rem(x + 3, 4), lax.rem(x + 2, 4)
    y_up, y_down, y_far = lax.rem(y + 1, 4), lax.rem(y + 3, 4), lax.rem(y + 2, 4)
    planes = (hi * 4, (1 - hi) * 4)
    around = (x, x_up, x_far, x_down)

    loads = [
        pltpu.make_async_copy(src, dst, load_sem.at[i])
        for i, (src, dst) in enumerate(
            (
                (latents_hbm, latents_ref),
                (scale_hbm, scale_ref),
                (uk_hbm, uk_ref),
                (lens_hbm, lens_ref),
                (uv_hbm, uv_ref),
                (q_hbm, q_ref),
            )
        )
    ]
    for load in loads:
        load.start()

    def place(a, b, c, d, e):
        return {"ctx": a * 8 + b * 2 + c, "head": d * 4 + e}

    to_x = (place(hi, x_up, core, lo, y), place(hi, x_down, core, lo, y))
    to_y = (place(hi, x, core, lo, y_up), place(hi, x, core, lo, y_down))
    to_z = place(1 - hi, x, core, 1 - lo, y)
    to_core = place(hi, x, 1 - core, lo, y)

    def copy(src, dst, ssem, rsem, target):
        return pltpu.make_async_remote_copy(
            src_ref=src, dst_ref=dst, send_sem=ssem, recv_sem=rsem,
            device_id=target, device_id_type=MESH,
        )

    pending = []

    def go(ref, ssem, rsem, target):
        one = copy(ref, ref, ssem, rsem, target)
        one.start()
        pending.append(one)

    def got(ref, ssem, rsem):
        copy(ref, ref, ssem, rsem, to_core).wait_recv()

    barrier = pltpu.get_barrier_semaphore()
    for target in (*to_x, *to_y, to_z, to_core):
        pl.semaphore_signal(barrier, inc=1, device_id=target, device_id_type=MESH)

    def block(plane, r):
        return planes[plane] + around[r]

    loads[0].wait()
    loads[1].wait()
    mine = block(0, 0)
    latent = latents_ref[...].astype(jnp.float32)
    keys_ref[mine, core, :, :LAT] = (latent[:LAT] * scale_ref[...]).T.astype(jnp.bfloat16)
    keys_ref[mine, core, :, LAT:] = latent[LAT:].T.astype(jnp.bfloat16)

    pl.semaphore_wait(barrier, 6)

    parts = (pl.ds(0, rows // 2), pl.ds(rows // 2, rows // 2))
    width = rows // 4

    def strip(index):
        return pl.ds(pl.multiple_of(index * width, 16), width)

    def strip_half(index, which):
        return pl.ds(pl.multiple_of(index * width + which * (width // 2), 16), width // 2)

    def at(plane, r, part):
        return keys_ref.at[block(plane, r), core, part]

    def to_sibling(plane, r):
        i = plane * 4 + r
        go(keys_ref.at[block(plane, r), core], csend.at[i], cgot.at[i], to_core)

    def from_sibling(plane, r):
        i = plane * 4 + r
        got(keys_ref.at[block(plane, r), 1 - core], csend.at[i], cgot.at[i])

    origin = (3, 1)

    def own_first():
        for d in range(2):
            go(at(0, 0, parts[d]), x1send.at[d], x1got.at[d], to_x[d])

    def own_second():
        for d in range(2):
            go(at(0, 0, parts[1 - d]), x1send.at[2 + d], x1got.at[2 + d], to_x[d])

    def near(turn, d):
        return at(0, origin[d], parts[d if turn == 0 else 1 - d])

    def half_to_sibling(turn):
        for d in range(2):
            i = turn * 2 + d
            go(near(turn, d), hsend.at[i], hgot.at[i], to_core)

    def half_from_sibling(turn):
        for d in range(2):
            i = turn * 2 + d
            ref = keys_ref.at[block(0, origin[d]), 1 - core, parts[d if turn == 0 else 1 - d]]
            got(ref, hsend.at[i], hgot.at[i])

    def own_onward():
        for d in range(2):
            got(near(0, d), x1send.at[d], x1got.at[d])
            go(near(0, d), x2send.at[d], x2got.at[d], to_x[d])
        half_to_sibling(0)

    def own_near():
        for d in range(2):
            got(near(1, d), x1send.at[2 + d], x1got.at[2 + d])
        half_to_sibling(1)

    def own_far():
        for d in range(2):
            got(at(0, 2, parts[d]), x2send.at[d], x2got.at[d])
        to_sibling(0, 2)

    def y_step1(r):
        for d in range(2):
            i = r * 2 + d
            go(at(1, r, strip(y)), y1send.at[i], y1got.at[i], to_y[d])

    def from_z():
        got(at(1, 0, strip(y)), zsend.at[0], zgot.at[0])
        for d in range(2):
            go(at(1, 0, strip(y)), s1send.at[d], s1got.at[d], to_x[d])
        y_step1(0)

    def strips_onward():
        for d in range(2):
            got(at(1, origin[d], strip(y)), s1send.at[d], s1got.at[d])
            go(at(1, origin[d], strip_half(y, d)), s2send.at[d], s2got.at[d], to_x[d])
        y_step1(1)
        y_step1(3)

    def strips_far():
        for d in range(2):
            got(at(1, 2, strip_half(y, d)), s2send.at[d], s2got.at[d])
        y_step1(2)

    def y_step2(r):
        for d, source in enumerate((y_down, y_up)):
            i = r * 2 + d
            got(at(1, r, strip(source)), y1send.at[i], y1got.at[i])
            go(at(1, r, strip_half(source, d)), y2send.at[i], y2got.at[i], to_y[d])

    def y_finish(r):
        for d in range(2):
            i = r * 2 + d
            got(at(1, r, strip_half(y_far, d)), y2send.at[i], y2got.at[i])
        to_sibling(1, r)

    def queries():
        for h in range(heads):
            q = q_ref[h].astype(jnp.float32).T.astype(jnp.bfloat16)
            lat = jnp.dot(q[:, :NOPE], uk_ref[h], preferred_element_type=jnp.float32)
            qf_ref[h, :, :LAT] = lat.astype(jnp.bfloat16)
            qf_ref[h, :, LAT:] = q[:, NOPE:]

    go(at(0, 0, strip(y)), zsend.at[0], zgot.at[0], to_z)
    own_first()
    to_sibling(0, 0)
    loads[2].wait()
    loads[5].wait()
    queries()
    from_z()
    own_second()

    loads[3].wait()
    t0 = ctx * rows
    qpos = t0 + lax.broadcasted_iota(jnp.int32, (rows, 128), 0)
    first = jnp.zeros_like(qpos)
    end = jnp.int32(0)
    for k in range(lens_ref.shape[0]):
        end = end + lens_ref[k]
        first = jnp.where(qpos >= end, end, first)
    first_ref[...] = jnp.concatenate([first] * GROUP, axis=0)
    m_ref[...] = jnp.full_like(m_ref, NEG)

    lane_iota = lax.broadcasted_iota(jnp.int32, (1, 128), 1)

    def scores(pieces, whole, diagonal=False):
        def one_group(g, carry):
            q = qf_ref[pl.ds(g * GROUP, GROUP)].reshape(block_rows, -1)
            if whole:
                keys = keys_ref[pieces[0][0], pieces[0][1]]
            else:
                keys = jnp.concatenate([keys_ref[p, k, parts[part]] for p, k, part in pieces], axis=0)
            s = lax.dot_general(
                q, keys, (((1,), (1,)), ((), ())), preferred_element_type=jnp.float32
            )
            here = pl.ds(pl.multiple_of(g * block_rows, block_rows), block_rows)
            top = m_ref[here]
            for n, (p, k, part) in enumerate(pieces):
                j = p * 2 + k
                lane = part * (rows // 2)
                base = jnp.where(j <= ctx, j * rows + lane, -TOO_FAR)
                allowed = first_ref[...] <= base + lane_iota
                if diagonal:
                    local = lax.broadcasted_iota(jnp.int32, (block_rows, 128), 0)
                    ahead = lane + lax.broadcasted_iota(jnp.int32, (block_rows, 128), 1)
                    allowed = allowed & (ahead <= lax.rem(local, rows))
                one = jnp.where(allowed, s[:, n * 128 : (n + 1) * 128], NEG)
                s_ref[j, here, lane : lane + 128] = one
                top = jnp.maximum(top, one)
            m_ref[here] = top
            return carry

        lax.fori_loop(0, groups, one_group, 0)

    def near_tile(turn, k):
        below, above = block(0, origin[0]), block(0, origin[1])

        @pl.when((below * 2 + k < ctx) | (above * 2 + k < ctx))
        def _():
            scores(((below, k, turn), (above, k, 1 - turn)), False)

    def tiles(plane, r, count, k):
        def one(i, carry):
            p = planes[plane] + lax.rem(x + r + 2 * i, 4)

            @pl.when(p * 2 + k < ctx)
            def _():
                scores(((p, k, 0), (p, k, 1)), True)

            return carry

        lax.fori_loop(0, count, one, 0)

    scores(((mine, core, 0), (mine, core, 1)), True, True)
    from_sibling(0, 0)
    tiles(0, 0, 1, 1 - core)
    strips_onward()
    own_onward()
    near_tile(0, core)
    y_step2(0)
    half_from_sibling(0)
    near_tile(0, 1 - core)
    own_near()
    strips_far()
    near_tile(1, core)
    y_step2(1)
    y_step2(3)
    y_finish(0)
    half_from_sibling(1)
    near_tile(1, 1 - core)
    own_far()
    y_step2(2)
    tiles(1, 0, 1, core)
    tiles(0, 2, 1, core)
    y_finish(1)
    y_finish(3)
    from_sibling(1, 0)
    tiles(1, 0, 1, 1 - core)
    y_finish(2)
    tiles(1, 1, 2, core)
    from_sibling(0, 2)
    tiles(0, 2, 1, 1 - core)
    from_sibling(1, 1)
    from_sibling(1, 3)
    tiles(1, 1, 2, 1 - core)
    tiles(1, 2, 1, core)
    from_sibling(1, 2)
    tiles(1, 2, 1, 1 - core)

    chunks = ctx // 4 + 1

    def clear(j, carry):
        s_ref[j] = jnp.full(s_ref.shape[1:], NEG, jnp.float32)
        return carry

    lax.fori_loop(ctx + 1, chunks * 4, clear, 0)

    loads[4].wait()

    def context_of(g, carry):
        here = pl.ds(pl.multiple_of(g * block_rows, block_rows), block_rows)
        m = jnp.max(m_ref[here], axis=1, keepdims=True)
        m_ref[here] = jnp.broadcast_to(m, (block_rows, 128))
        l_ref[...] = jnp.zeros_like(l_ref)
        acc_ref[...] = jnp.zeros_like(acc_ref)

        def weigh(p, carry):
            top = m_ref[here]
            weights = []
            total = l_ref[...]
            for k in range(4):
                for lane in range(0, rows, 128):
                    s = s_ref[4 * p + k, here, lane : lane + 128]
                    w = jnp.exp2((s - top) * EXP_SCALE)
                    total = total + w
                    weights.append(w.astype(jnp.bfloat16))
            l_ref[...] = total
            values = keys_ref[pl.ds(2 * p, 2), :, :, :LAT].reshape(4 * rows, LAT)
            acc_ref[...] += jnp.dot(
                jnp.concatenate(weights, axis=1), values, preferred_element_type=jnp.float32
            )
            return carry

        lax.fori_loop(0, chunks, weigh, 0)
        inverse = 1.0 / jnp.sum(l_ref[...], axis=1, keepdims=True)
        context = (acc_ref[...] * inverse).astype(jnp.bfloat16)
        for i in range(GROUP):
            h = g * GROUP + i
            one = jnp.dot(
                context[i * rows : (i + 1) * rows], uv_ref[h], preferred_element_type=jnp.float32
            )
            out_ref[:, pl.ds(pl.multiple_of(h * VDIM, VDIM), VDIM)] = one.astype(jnp.bfloat16)
        return carry

    lax.fori_loop(0, groups, context_of, 0)
    for one in pending:
        one.wait_send()


def attend(doc_lengths, by_head, latents, scale_row, w_uk, w_uv):
    heads, _, rows = by_head.shape
    width = latents.shape[0]
    dma = pltpu.SemaphoreType.DMA
    vmem = pltpu.VMEM
    outside = pl.BlockSpec(memory_space=pl.ANY)
    whole = pl.BlockSpec(memory_space=pltpu.VMEM)
    block_rows = GROUP * rows
    return pl.pallas_call(
        attend_kernel,
        out_shape=jax.ShapeDtypeStruct((rows, heads * VDIM), jnp.bfloat16),
        in_specs=[outside] * 6,
        out_specs=whole,
        scratch_shapes=[
            pltpu.SMEM(doc_lengths.shape, jnp.int32),
            vmem(by_head.shape, by_head.dtype),
            vmem(latents.shape, latents.dtype),
            vmem(scale_row.shape, scale_row.dtype),
            vmem(w_uk.shape, w_uk.dtype),
            vmem(w_uv.shape, w_uv.dtype),
            vmem((8, 2, rows, width), jnp.bfloat16),
            vmem((heads, rows, width), jnp.bfloat16),
            vmem((16, heads * rows, rows), jnp.float32),
            vmem((heads * rows, 128), jnp.float32),
            vmem((block_rows, 128), jnp.float32),
            vmem((block_rows, LAT), jnp.float32),
            vmem((block_rows, 128), jnp.int32),
            dma((6,)),
            dma((1,)), dma((1,)),
            dma((4,)), dma((4,)),
            dma((2,)), dma((2,)),
            dma((2,)), dma((2,)),
            dma((2,)), dma((2,)),
            dma((8,)), dma((8,)),
            dma((8,)), dma((8,)),
            dma((8,)), dma((8,)),
            dma((4,)), dma((4,)),
        ],
        compiler_params=pltpu.CompilerParams(
            collective_id=1, has_side_effects=True, vmem_limit_bytes=61 << 20
        ),
        name="attend",
    )(doc_lengths, by_head, latents, scale_row, w_uk, w_uv)


def reduce_kernel(
    x_hbm, w_ref, out_ref, x_ref, x_sem, wbuf, own, zrecv, y1recv, y2recv, ysecond1, ysecond2, zlast,
    wsem, zsend, zgot, y1send, y1got, y2send, y2got, s1send, s1got, s2send, s2got, lsend, lgot,
):
    cols = out_ref.shape[1]
    half = out_ref.shape[0] // 2
    quarter = half // 2
    me = lax.axis_index("head")
    y = lax.rem(me, 4)
    z = me // 4
    up = z * 4 + lax.rem(y + 1, 4)
    down = z * 4 + lax.rem(y + 3, 4)
    across = (1 - z) * 4 + y
    blocks = ((2, 0), (2, 1), (1, 0), (3, 0), (1, 1), (3, 1), (0, 0), (0, 1))
    slot = {key: k for k, key in enumerate(blocks)}
    first = pl.ds(0, half)
    second = pl.ds(half, half)

    def fetch(k):
        shift, mine = blocks[k]
        plane = z if mine else 1 - z
        start = pl.multiple_of((plane * 4 + lax.rem(y + shift, 4)) * cols, 128)
        return pltpu.make_async_copy(w_ref.at[:, pl.ds(start, cols)], wbuf.at[k], wsem.at[k])

    def send(src, dst, ssem, rsem, target):
        return pltpu.make_async_remote_copy(
            src_ref=src, dst_ref=dst, send_sem=ssem, recv_sem=rsem,
            device_id={"head": target}, device_id_type=MESH,
        )

    load = pltpu.make_async_copy(x_hbm, x_ref, x_sem.at[0])
    load.start()
    for k in range(2):
        fetch(k).start()
    barrier = pltpu.get_barrier_semaphore()
    for target in (up, down, across):
        pl.semaphore_signal(barrier, inc=1, device_id={"head": target}, device_id_type=MESH)
    load.wait()

    pending = []

    def go(copy):
        copy.start()
        pending.append(copy)

    def across_copy(i, k):
        return send(own.at[k, first], zrecv.at[i], zsend.at[i], zgot.at[i], across)

    def step1(k, base, buf, ssem, rsem, i):
        go(send(own.at[k, pl.ds(base, quarter)], buf.at[i], ssem.at[i], rsem.at[i], up))
        go(
            send(
                own.at[k, pl.ds(base + quarter, quarter)],
                buf.at[i + 1], ssem.at[i + 1], rsem.at[i + 1], down,
            )
        )

    across_order = (2, 1, 3, 0)
    across_copies = {}

    def compute(k):
        fetch(k).wait()
        if k + 2 < 8:
            fetch(k + 2).start()
        own[k] = jnp.dot(x_ref[...], wbuf[k], preferred_element_type=jnp.float32).astype(
            jnp.bfloat16
        )
        if k == 0:
            pl.semaphore_wait(barrier, 3)
        shift, mine = blocks[k]
        if not mine:
            i = across_order.index(shift)
            across_copies[i] = across_copy(i, k)
            go(across_copies[i])
        if shift == 2:
            step1(k, half, y1recv, y1send, y1got, 2 * mine)

    def add_rows(k, rows, *terms):
        total = own[k, rows].astype(jnp.float32)
        for term in terms:
            total = total + term.astype(jnp.float32)
        return total

    copies = {}

    def y_first_step2(mine):
        for side, (shift, target, offset) in enumerate(((1, up, 0), (3, down, quarter))):
            k = slot[(shift, mine)]
            i = 2 * mine + side
            rows = pl.ds(half + offset, quarter)
            send(
                own.at[0, pl.ds(0, quarter)], y1recv.at[i], y1send.at[i], y1got.at[i], target
            ).wait_recv()
            own[k, rows] = add_rows(k, rows, y1recv[i]).astype(jnp.bfloat16)
            go(send(own.at[k, second], y2recv.at[i], y2send.at[i], y2got.at[i], target))

    def got(buf, i, ssem, rsem, rows):
        send(own.at[0, pl.ds(0, rows)], buf.at[i], ssem.at[i], rsem.at[i], across).wait_recv()

    for k in range(6):
        compute(k)
    y_first_step2(0)
    compute(6)

    got(zrecv, 0, zsend, zgot, half)
    k = slot[(2, 1)]
    own[k, first] = add_rows(k, first, zrecv[0]).astype(jnp.bfloat16)
    step1(k, 0, ysecond1, s1send, s1got, 0)

    compute(7)
    y_first_step2(1)

    got(y2recv, 0, y2send, y2got, half)
    got(y2recv, 1, y2send, y2got, half)
    k = slot[(0, 0)]
    own[k, second] = add_rows(k, second, y2recv[0], y2recv[1]).astype(jnp.bfloat16)
    go(send(own.at[k, second], zlast.at[0], lsend.at[0], lgot.at[0], across))

    for side, (shift, target, offset) in enumerate(((1, up, 0), (3, down, quarter))):
        k = slot[(shift, 1)]
        got(zrecv, 1 + side, zsend, zgot, half)
        got(ysecond1, side, s1send, s1got, quarter)
        own[k, first] = add_rows(k, first, zrecv[1 + side]).astype(jnp.bfloat16)
        rows = pl.ds(offset, quarter)
        own[k, rows] = add_rows(k, rows, ysecond1[side]).astype(jnp.bfloat16)
        go(send(own.at[k, first], ysecond2.at[side], s2send.at[side], s2got.at[side], target))

    k = slot[(0, 1)]
    got(y2recv, 2, y2send, y2got, half)
    got(y2recv, 3, y2send, y2got, half)
    got(zlast, 0, lsend, lgot, half)
    out_ref[second] = add_rows(k, second, y2recv[2], y2recv[3], zlast[0]).astype(jnp.bfloat16)
    got(zrecv, 3, zsend, zgot, half)
    got(ysecond2, 0, s2send, s2got, half)
    got(ysecond2, 1, s2send, s2got, half)
    out_ref[first] = add_rows(k, first, zrecv[3], ysecond2[0], ysecond2[1]).astype(jnp.bfloat16)
    for copy in pending:
        copy.wait_send()


def project_and_reduce(head_out, w_o):
    rows, inner = head_out.shape
    cols = w_o.shape[1] // 8
    half = rows // 2
    dma = pltpu.SemaphoreType.DMA
    return pl.pallas_call(
        reduce_kernel,
        out_shape=jax.ShapeDtypeStruct((rows, cols), jnp.bfloat16),
        in_specs=[pl.BlockSpec(memory_space=pltpu.HBM)] * 2,
        out_specs=pl.BlockSpec(memory_space=pltpu.VMEM),
        scratch_shapes=[
            pltpu.VMEM((rows, inner), jnp.bfloat16),
            dma((1,)),
            pltpu.VMEM((8, inner, cols), jnp.bfloat16),
            pltpu.VMEM((8, rows, cols), jnp.bfloat16),
            pltpu.VMEM((4, half, cols), jnp.bfloat16),
            pltpu.VMEM((4, half // 2, cols), jnp.bfloat16),
            pltpu.VMEM((4, half, cols), jnp.bfloat16),
            pltpu.VMEM((2, half // 2, cols), jnp.bfloat16),
            pltpu.VMEM((2, half, cols), jnp.bfloat16),
            pltpu.VMEM((1, half, cols), jnp.bfloat16),
            dma((8,)),
            dma((4,)), dma((4,)),
            dma((4,)), dma((4,)),
            dma((4,)), dma((4,)),
            dma((2,)), dma((2,)),
            dma((2,)), dma((2,)),
            dma((1,)), dma((1,)),
        ],
        compiler_params=pltpu.CompilerParams(
            collective_id=0, has_side_effects=True, vmem_limit_bytes=62 << 20
        ),
        name="project_and_reduce",
    )(head_out, w_o)


def shards(query, latents, lat_scale, doc_lengths, w_uk, w_uv, w_o):
    by_head = jnp.transpose(query, (1, 2, 0))
    head_out = attend(doc_lengths, by_head, latents.T, lat_scale.reshape(1, -1), w_uk, w_uv)
    return project_and_reduce(head_out, w_o)


def solution(mesh):
    placed = (
        P("ctx", "head", None),
        P("ctx", None),
        P("ctx"),
        P(),
        P("head", None, None),
        P("head", None, None),
        P("head", None),
    )
    return jax.shard_map(
        shards, mesh=mesh, in_specs=placed, out_specs=P("ctx", "head"), check_vma=False
    )
```

```python
import jax
import jax.numpy as jnp
from jax import lax
from jax.experimental import pallas as pl
from jax.experimental.pallas import tpu as pltpu
from jax.sharding import PartitionSpec as P

LAT = 512
NOPE = 128
QDIM = 192
VDIM = 128
GROUP = 8
NEG = -1e30
TOO_FAR = 1 << 20
MESH = pl.DeviceIdType.MESH
EXP_SCALE = float(QDIM) ** -0.5 * 1.4426950408889634


def attend_kernel(
    lens_hbm, q_hbm, latents_hbm, scale_hbm, uk_hbm, uv_hbm, out_ref,
    lens_ref, q_ref, latents_ref, scale_ref, uk_ref, uv_ref,
    keys_ref, qf_ref, s_ref, m_ref, l_ref, acc_ref, first_ref, load_sem,
    zsend, zgot, x1send, x1got, x2send, x2got, s1send, s1got, s2send, s2got,
    y1send, y1got, y2send, y2got, csend, cgot, hsend, hgot,
):
    rows = latents_ref.shape[1]
    heads = q_ref.shape[0]
    block_rows = GROUP * rows
    groups = heads // GROUP
    ctx = lax.axis_index("ctx")
    head = lax.axis_index("head")
    core = lax.rem(ctx, 2)
    x = lax.rem(ctx // 2, 4)
    hi = ctx // 8
    y = lax.rem(head, 4)
    lo = head // 4
    x_up, x_down, x_far = lax.rem(x + 1, 4), lax.rem(x + 3, 4), lax.rem(x + 2, 4)
    y_up, y_down, y_far = lax.rem(y + 1, 4), lax.rem(y + 3, 4), lax.rem(y + 2, 4)
    planes = (hi * 4, (1 - hi) * 4)
    around = (x, x_up, x_far, x_down)

    loads = [
        pltpu.make_async_copy(src, dst, load_sem.at[i])
        for i, (src, dst) in enumerate(
            (
                (latents_hbm, latents_ref),
                (scale_hbm, scale_ref),
                (uk_hbm, uk_ref),
                (lens_hbm, lens_ref),
                (uv_hbm, uv_ref),
                (q_hbm, q_ref),
            )
        )
    ]
    for load in loads:
        load.start()

    def place(a, b, c, d, e):
        return {"ctx": a * 8 + b * 2 + c, "head": d * 4 + e}

    to_x = (place(hi, x_up, core, lo, y), place(hi, x_down, core, lo, y))
    to_y = (place(hi, x, core, lo, y_up), place(hi, x, core, lo, y_down))
    to_z = place(1 - hi, x, core, 1 - lo, y)
    to_core = place(hi, x, 1 - core, lo, y)

    def copy(src, dst, ssem, rsem, target):
        return pltpu.make_async_remote_copy(
            src_ref=src, dst_ref=dst, send_sem=ssem, recv_sem=rsem,
            device_id=target, device_id_type=MESH,
        )

    pending = []

    def go(ref, ssem, rsem, target):
        one = copy(ref, ref, ssem, rsem, target)
        one.start()
        pending.append(one)

    def got(ref, ssem, rsem):
        copy(ref, ref, ssem, rsem, to_core).wait_recv()

    barrier = pltpu.get_barrier_semaphore()
    for target in (*to_x, *to_y, to_z, to_core):
        pl.semaphore_signal(barrier, inc=1, device_id=target, device_id_type=MESH)

    def block(plane, r):
        return planes[plane] + around[r]

    loads[0].wait()
    loads[1].wait()
    mine = block(0, 0)
    latent = latents_ref[...].astype(jnp.float32)
    keys_ref[mine, core, :, :LAT] = (latent[:LAT] * scale_ref[...]).T.astype(jnp.bfloat16)
    keys_ref[mine, core, :, LAT:] = latent[LAT:].T.astype(jnp.bfloat16)

    pl.semaphore_wait(barrier, 6)

    parts = (pl.ds(0, rows // 2), pl.ds(rows // 2, rows // 2))
    width = rows // 4

    def strip(index):
        return pl.ds(pl.multiple_of(index * width, 16), width)

    def strip_half(index, which):
        return pl.ds(pl.multiple_of(index * width + which * (width // 2), 16), width // 2)

    def at(plane, r, part):
        return keys_ref.at[block(plane, r), core, part]

    def to_sibling(plane, r):
        i = plane * 4 + r
        go(keys_ref.at[block(plane, r), core], csend.at[i], cgot.at[i], to_core)

    def from_sibling(plane, r):
        i = plane * 4 + r
        got(keys_ref.at[block(plane, r), 1 - core], csend.at[i], cgot.at[i])

    origin = (3, 1)

    def own_first():
        for d in range(2):
            go(at(0, 0, parts[d]), x1send.at[d], x1got.at[d], to_x[d])

    def own_second():
        for d in range(2):
            go(at(0, 0, parts[1 - d]), x1send.at[2 + d], x1got.at[2 + d], to_x[d])

    def near(turn, d):
        return at(0, origin[d], parts[d if turn == 0 else 1 - d])

    def half_to_sibling(turn):
        for d in range(2):
            i = turn * 2 + d
            go(near(turn, d), hsend.at[i], hgot.at[i], to_core)

    def half_from_sibling(turn):
        for d in range(2):
            i = turn * 2 + d
            ref = keys_ref.at[block(0, origin[d]), 1 - core, parts[d if turn == 0 else 1 - d]]
            got(ref, hsend.at[i], hgot.at[i])

    def own_onward():
        for d in range(2):
            got(near(0, d), x1send.at[d], x1got.at[d])
            go(near(0, d), x2send.at[d], x2got.at[d], to_x[d])
        half_to_sibling(0)

    def own_near():
        for d in range(2):
            got(near(1, d), x1send.at[2 + d], x1got.at[2 + d])
        half_to_sibling(1)

    def own_far():
        for d in range(2):
            got(at(0, 2, parts[d]), x2send.at[d], x2got.at[d])
        to_sibling(0, 2)

    def y_step1(r):
        for d in range(2):
            i = r * 2 + d
            go(at(1, r, strip(y)), y1send.at[i], y1got.at[i], to_y[d])

    def from_z():
        got(at(1, 0, strip(y)), zsend.at[0], zgot.at[0])
        for d in range(2):
            go(at(1, 0, strip(y)), s1send.at[d], s1got.at[d], to_x[d])
        y_step1(0)

    def strips_onward():
        for d in range(2):
            got(at(1, origin[d], strip(y)), s1send.at[d], s1got.at[d])
            go(at(1, origin[d], strip_half(y, d)), s2send.at[d], s2got.at[d], to_x[d])
        y_step1(1)
        y_step1(3)

    def strips_far():
        for d in range(2):
            got(at(1, 2, strip_half(y, d)), s2send.at[d], s2got.at[d])
        y_step1(2)

    def y_step2(r):
        for d, source in enumerate((y_down, y_up)):
            i = r * 2 + d
            got(at(1, r, strip(source)), y1send.at[i], y1got.at[i])
            go(at(1, r, strip_half(source, d)), y2send.at[i], y2got.at[i], to_y[d])

    def y_finish(r):
        for d in range(2):
            i = r * 2 + d
            got(at(1, r, strip_half(y_far, d)), y2send.at[i], y2got.at[i])
        to_sibling(1, r)

    def queries():
        for h in range(heads):
            q = q_ref[h].astype(jnp.float32).T.astype(jnp.bfloat16)
            lat = jnp.dot(q[:, :NOPE], uk_ref[h], preferred_element_type=jnp.float32)
            qf_ref[h, :, :LAT] = lat.astype(jnp.bfloat16)
            qf_ref[h, :, LAT:] = q[:, NOPE:]

    go(at(0, 0, strip(y)), zsend.at[0], zgot.at[0], to_z)
    own_first()
    to_sibling(0, 0)
    loads[2].wait()
    loads[5].wait()
    queries()
    from_z()
    own_second()

    loads[3].wait()
    t0 = ctx * rows
    qpos = t0 + lax.broadcasted_iota(jnp.int32, (rows, 128), 0)
    first = jnp.zeros_like(qpos)
    end = jnp.int32(0)
    for k in range(lens_ref.shape[0]):
        end = end + lens_ref[k]
        first = jnp.where(qpos >= end, end, first)
    first_ref[...] = jnp.concatenate([first] * GROUP, axis=0)
    m_ref[...] = jnp.full_like(m_ref, NEG)

    lane_iota = lax.broadcasted_iota(jnp.int32, (1, 128), 1)

    def scores(pieces, whole, diagonal=False):
        def one_group(g, carry):
            q = qf_ref[pl.ds(g * GROUP, GROUP)].reshape(block_rows, -1)
            if whole:
                keys = keys_ref[pieces[0][0], pieces[0][1]]
            else:
                keys = jnp.concatenate([keys_ref[p, k, parts[part]] for p, k, part in pieces], axis=0)
            s = lax.dot_general(
                q, keys, (((1,), (1,)), ((), ())), preferred_element_type=jnp.float32
            )
            here = pl.ds(pl.multiple_of(g * block_rows, block_rows), block_rows)
            top = m_ref[here]
            for n, (p, k, part) in enumerate(pieces):
                j = p * 2 + k
                lane = part * (rows // 2)
                base = jnp.where(j <= ctx, j * rows + lane, -TOO_FAR)
                allowed = first_ref[...] <= base + lane_iota
                if diagonal:
                    local = lax.broadcasted_iota(jnp.int32, (block_rows, 128), 0)
                    ahead = lane + lax.broadcasted_iota(jnp.int32, (block_rows, 128), 1)
                    allowed = allowed & (ahead <= lax.rem(local, rows))
                one = jnp.where(allowed, s[:, n * 128 : (n + 1) * 128], NEG)
                s_ref[j, here, lane : lane + 128] = one
                top = jnp.maximum(top, one)
            m_ref[here] = top
            return carry

        lax.fori_loop(0, groups, one_group, 0)

    def near_tile(turn, k):
        below, above = block(0, origin[0]), block(0, origin[1])

        @pl.when((below * 2 + k < ctx) | (above * 2 + k < ctx))
        def _():
            scores(((below, k, turn), (above, k, 1 - turn)), False)

    def tiles(plane, r, count, k):
        def one(i, carry):
            p = planes[plane] + lax.rem(x + r + 2 * i, 4)

            @pl.when(p * 2 + k < ctx)
            def _():
                scores(((p, k, 0), (p, k, 1)), True)

            return carry

        lax.fori_loop(0, count, one, 0)

    scores(((mine, core, 0), (mine, core, 1)), True, True)
    from_sibling(0, 0)
    tiles(0, 0, 1, 1 - core)
    strips_onward()
    own_onward()
    near_tile(0, core)
    y_step2(0)
    half_from_sibling(0)
    near_tile(0, 1 - core)
    own_near()
    strips_far()
    near_tile(1, core)
    y_step2(1)
    y_step2(3)
    y_finish(0)
    half_from_sibling(1)
    near_tile(1, 1 - core)
    own_far()
    y_step2(2)
    tiles(1, 0, 1, core)
    tiles(0, 2, 1, core)
    y_finish(1)
    y_finish(3)
    from_sibling(1, 0)
    tiles(1, 0, 1, 1 - core)
    y_finish(2)
    tiles(1, 1, 2, core)
    from_sibling(0, 2)
    tiles(0, 2, 1, 1 - core)
    from_sibling(1, 1)
    from_sibling(1, 3)
    tiles(1, 1, 2, 1 - core)
    tiles(1, 2, 1, core)
    from_sibling(1, 2)
    tiles(1, 2, 1, 1 - core)

    chunks = ctx // 4 + 1

    def clear(j, carry):
        s_ref[j] = jnp.full(s_ref.shape[1:], NEG, jnp.float32)
        return carry

    lax.fori_loop(ctx + 1, chunks * 4, clear, 0)

    loads[4].wait()

    def context_of(g, carry):
        here = pl.ds(pl.multiple_of(g * block_rows, block_rows), block_rows)
        m = jnp.max(m_ref[here], axis=1, keepdims=True)
        m_ref[here] = jnp.broadcast_to(m, (block_rows, 128))
        l_ref[...] = jnp.zeros_like(l_ref)
        acc_ref[...] = jnp.zeros_like(acc_ref)

        def weigh(p, carry):
            top = m_ref[here]
            weights = []
            total = l_ref[...]
            for k in range(4):
                for lane in range(0, rows, 128):
                    s = s_ref[4 * p + k, here, lane : lane + 128]
                    w = jnp.exp2((s - top) * EXP_SCALE)
                    total = total + w
                    weights.append(w.astype(jnp.bfloat16))
            l_ref[...] = total
            values = keys_ref[pl.ds(2 * p, 2), :, :, :LAT].reshape(4 * rows, LAT)
            acc_ref[...] += jnp.dot(
                jnp.concatenate(weights, axis=1), values, preferred_element_type=jnp.float32
            )
            return carry

        lax.fori_loop(0, chunks, weigh, 0)
        inverse = 1.0 / jnp.sum(l_ref[...], axis=1, keepdims=True)
        context = (acc_ref[...] * inverse).astype(jnp.bfloat16)
        for i in range(GROUP):
            h = g * GROUP + i
            one = jnp.dot(
                context[i * rows : (i + 1) * rows], uv_ref[h], preferred_element_type=jnp.float32
            )
            out_ref[:, pl.ds(pl.multiple_of(h * VDIM, VDIM), VDIM)] = one.astype(jnp.bfloat16)
        return carry

    lax.fori_loop(0, groups, context_of, 0)
    for one in pending:
        one.wait_send()


def attend(doc_lengths, by_head, latents, scale_row, w_uk, w_uv):
    heads, _, rows = by_head.shape
    width = latents.shape[0]
    dma = pltpu.SemaphoreType.DMA
    vmem = pltpu.VMEM
    outside = pl.BlockSpec(memory_space=pl.ANY)
    whole = pl.BlockSpec(memory_space=pltpu.VMEM)
    block_rows = GROUP * rows
    return pl.pallas_call(
        attend_kernel,
        out_shape=jax.ShapeDtypeStruct((rows, heads * VDIM), jnp.bfloat16),
        in_specs=[outside] * 6,
        out_specs=whole,
        scratch_shapes=[
            pltpu.SMEM(doc_lengths.shape, jnp.int32),
            vmem(by_head.shape, by_head.dtype),
            vmem(latents.shape, latents.dtype),
            vmem(scale_row.shape, scale_row.dtype),
            vmem(w_uk.shape, w_uk.dtype),
            vmem(w_uv.shape, w_uv.dtype),
            vmem((8, 2, rows, width), jnp.bfloat16),
            vmem((heads, rows, width), jnp.bfloat16),
            vmem((16, heads * rows, rows), jnp.float32),
            vmem((heads * rows, 128), jnp.float32),
            vmem((block_rows, 128), jnp.float32),
            vmem((block_rows, LAT), jnp.float32),
            vmem((block_rows, 128), jnp.int32),
            dma((6,)),
            dma((1,)), dma((1,)),
            dma((4,)), dma((4,)),
            dma((2,)), dma((2,)),
            dma((2,)), dma((2,)),
            dma((2,)), dma((2,)),
            dma((8,)), dma((8,)),
            dma((8,)), dma((8,)),
            dma((8,)), dma((8,)),
            dma((4,)), dma((4,)),
        ],
        compiler_params=pltpu.CompilerParams(
            collective_id=1, has_side_effects=True, vmem_limit_bytes=61 << 20
        ),
        name="attend",
    )(doc_lengths, by_head, latents, scale_row, w_uk, w_uv)


def reduce_kernel(
    x_hbm, w_ref, out_ref, x_ref, x_sem, wbuf, own, zrecv, y1recv, y2recv, ysecond1, ysecond2, zlast,
    wsem, zsend, zgot, y1send, y1got, y2send, y2got, s1send, s1got, s2send, s2got, lsend, lgot,
):
    cols = out_ref.shape[1]
    rows = out_ref.shape[0]
    early = rows * 7 // 16
    late = rows - early
    down_rows = rows // 4
    early_up = early - down_rows
    late_up = late - down_rows
    me = lax.axis_index("head")
    y = lax.rem(me, 4)
    z = me // 4
    up = z * 4 + lax.rem(y + 1, 4)
    down = z * 4 + lax.rem(y + 3, 4)
    across = (1 - z) * 4 + y
    blocks = ((2, 0), (2, 1), (1, 0), (3, 0), (1, 1), (3, 1), (0, 0), (0, 1))
    slot = {key: k for k, key in enumerate(blocks)}
    first = pl.ds(0, early)
    second = pl.ds(early, late)

    def fetch(k):
        shift, mine = blocks[k]
        plane = z if mine else 1 - z
        start = pl.multiple_of((plane * 4 + lax.rem(y + shift, 4)) * cols, 128)
        return pltpu.make_async_copy(w_ref.at[:, pl.ds(start, cols)], wbuf.at[k], wsem.at[k])

    def send(src, dst, ssem, rsem, target):
        return pltpu.make_async_remote_copy(
            src_ref=src, dst_ref=dst, send_sem=ssem, recv_sem=rsem,
            device_id={"head": target}, device_id_type=MESH,
        )

    load = pltpu.make_async_copy(x_hbm, x_ref, x_sem.at[0])
    load.start()
    for k in range(2):
        fetch(k).start()
    barrier = pltpu.get_barrier_semaphore()
    for target in (up, down, across):
        pl.semaphore_signal(barrier, inc=1, device_id={"head": target}, device_id_type=MESH)
    load.wait()

    pending = []

    def go(copy):
        copy.start()
        pending.append(copy)

    def across_copy(i, k):
        return send(own.at[k, first], zrecv.at[i], zsend.at[i], zgot.at[i], across)

    def step1(k, base, upper, buf, ssem, rsem, i):
        for n, target, start, count in (
            (i, up, base, upper),
            (i + 1, down, base + upper, down_rows),
        ):
            part = own.at[k, pl.ds(start, count)]
            go(send(part, buf.at[n, pl.ds(0, count)], ssem.at[n], rsem.at[n], target))

    across_order = (2, 1, 3, 0)
    across_copies = {}

    def compute(k):
        fetch(k).wait()
        if k + 2 < 8:
            fetch(k + 2).start()
        own[k] = jnp.dot(x_ref[...], wbuf[k], preferred_element_type=jnp.float32).astype(
            jnp.bfloat16
        )
        if k == 0:
            pl.semaphore_wait(barrier, 3)
        shift, mine = blocks[k]
        if not mine:
            i = across_order.index(shift)
            across_copies[i] = across_copy(i, k)
            go(across_copies[i])
        if shift == 2:
            step1(k, early, late_up, y1recv, y1send, y1got, 2 * mine)

    def add_rows(k, rows, *terms):
        total = own[k, rows].astype(jnp.float32)
        for term in terms:
            total = total + term.astype(jnp.float32)
        return total

    copies = {}

    def got(buf, i, ssem, rsem, count):
        send(
            own.at[0, pl.ds(0, count)], buf.at[i, pl.ds(0, count)], ssem.at[i], rsem.at[i], across
        ).wait_recv()

    def y_first_step2(mine):
        for side, (shift, target, offset, count) in enumerate(
            ((1, up, early, late_up), (3, down, early + late_up, down_rows))
        ):
            k = slot[(shift, mine)]
            i = 2 * mine + side
            part = pl.ds(offset, count)
            got(y1recv, i, y1send, y1got, count)
            own[k, part] = add_rows(k, part, y1recv[i, :count]).astype(jnp.bfloat16)
            go(send(own.at[k, second], y2recv.at[i], y2send.at[i], y2got.at[i], target))

    for k in range(6):
        compute(k)
    y_first_step2(0)
    compute(6)

    got(zrecv, 0, zsend, zgot, early)
    k = slot[(2, 1)]
    own[k, first] = add_rows(k, first, zrecv[0]).astype(jnp.bfloat16)
    step1(k, 0, early_up, ysecond1, s1send, s1got, 0)

    compute(7)
    y_first_step2(1)

    got(y2recv, 0, y2send, y2got, late)
    got(y2recv, 1, y2send, y2got, late)
    k = slot[(0, 0)]
    own[k, second] = add_rows(k, second, y2recv[0], y2recv[1]).astype(jnp.bfloat16)
    go(send(own.at[k, second], zlast.at[0], lsend.at[0], lgot.at[0], across))

    for side, (shift, target, offset, count) in enumerate(
        ((1, up, 0, early_up), (3, down, early_up, down_rows))
    ):
        k = slot[(shift, 1)]
        got(zrecv, 1 + side, zsend, zgot, early)
        got(ysecond1, side, s1send, s1got, count)
        own[k, first] = add_rows(k, first, zrecv[1 + side]).astype(jnp.bfloat16)
        part = pl.ds(offset, count)
        own[k, part] = add_rows(k, part, ysecond1[side, :count]).astype(jnp.bfloat16)
        go(send(own.at[k, first], ysecond2.at[side], s2send.at[side], s2got.at[side], target))

    k = slot[(0, 1)]
    got(y2recv, 2, y2send, y2got, late)
    got(y2recv, 3, y2send, y2got, late)
    got(zlast, 0, lsend, lgot, late)
    out_ref[second] = add_rows(k, second, y2recv[2], y2recv[3], zlast[0]).astype(jnp.bfloat16)
    got(zrecv, 3, zsend, zgot, early)
    got(ysecond2, 0, s2send, s2got, early)
    got(ysecond2, 1, s2send, s2got, early)
    out_ref[first] = add_rows(k, first, zrecv[3], ysecond2[0], ysecond2[1]).astype(jnp.bfloat16)
    for copy in pending:
        copy.wait_send()


def project_and_reduce(head_out, w_o):
    rows, inner = head_out.shape
    cols = w_o.shape[1] // 8
    early = rows * 7 // 16
    late = rows - early
    late_up = late - rows // 4
    dma = pltpu.SemaphoreType.DMA
    return pl.pallas_call(
        reduce_kernel,
        out_shape=jax.ShapeDtypeStruct((rows, cols), jnp.bfloat16),
        in_specs=[pl.BlockSpec(memory_space=pltpu.HBM)] * 2,
        out_specs=pl.BlockSpec(memory_space=pltpu.VMEM),
        scratch_shapes=[
            pltpu.VMEM((rows, inner), jnp.bfloat16),
            dma((1,)),
            pltpu.VMEM((8, inner, cols), jnp.bfloat16),
            pltpu.VMEM((8, rows, cols), jnp.bfloat16),
            pltpu.VMEM((4, early, cols), jnp.bfloat16),
            pltpu.VMEM((4, late_up, cols), jnp.bfloat16),
            pltpu.VMEM((4, late, cols), jnp.bfloat16),
            pltpu.VMEM((2, rows // 4, cols), jnp.bfloat16),
            pltpu.VMEM((2, early, cols), jnp.bfloat16),
            pltpu.VMEM((1, late, cols), jnp.bfloat16),
            dma((8,)),
            dma((4,)), dma((4,)),
            dma((4,)), dma((4,)),
            dma((4,)), dma((4,)),
            dma((2,)), dma((2,)),
            dma((2,)), dma((2,)),
            dma((1,)), dma((1,)),
        ],
        compiler_params=pltpu.CompilerParams(
            collective_id=0, has_side_effects=True, vmem_limit_bytes=62 << 20
        ),
        name="project_and_reduce",
    )(head_out, w_o)


def shards(query, latents, lat_scale, doc_lengths, w_uk, w_uv, w_o):
    by_head = jnp.transpose(query, (1, 2, 0))
    head_out = attend(doc_lengths, by_head, latents.T, lat_scale.reshape(1, -1), w_uk, w_uv)
    return project_and_reduce(head_out, w_o)


def solution(mesh):
    placed = (
        P("ctx", "head", None),
        P("ctx", None),
        P("ctx"),
        P(),
        P("head", None, None),
        P("head", None, None),
        P("head", None),
    )
    return jax.shard_map(
        shards, mesh=mesh, in_specs=placed, out_specs=P("ctx", "head"), check_vma=False
    )
```
